512 devices in a mesh: mem: 32 (over z, core), space: 16 (over y, x).
Axes of the slice: x: 4, y: 4, z: 16, core: 2. Of those that a mesh axis runs over, the one named last changes fastest.
Arguments:
- ensemble: bfloat16 [1024, 262144], P('mem', 'space'), may hold values from -420 to 420, as said below
- log_weights: float32 [1024], replicated, may hold values from -405 to -195, as said below
Outputs:
- analysis: bfloat16 [1024, 262144], P('mem', 'space')
The draws below stay inside these ranges and needn't reach their ends.
Inputs may be any that keep to these rules, and one draw needn't show every extreme that they name: `ensemble`: finite values. `log_weights`: unnormalized log-likelihoods; only differences between members matter.
All inputs are finite; a program needn't handle non-finite values.
Results may differ from the reference program's by a relative error of at most 0.003.
The reference program's roundings to bfloat16 on the way (of `coupling`) count: a program that leaves them out, or rounds other values in their place, can miss the bound.
Values may be sent and summed in bfloat16 or wider, within the bound.
No kernel may reach another device: no remote copies, remote signals or barrier semaphores. Data moves between devices by JAX's collectives and lax.ppermute only.
A program may use at most 64 MiB of HBM per device.

```python
import math
import jax
import jax.numpy as jnp
from jax import lax

M = 1024
CELL_DEV = 16384
ITERS = 10
CELLS = 262144
N_SPACE = 16


def draw_ensemble(key, part):
    keys = jax.random.split(key, 5)
    spread = jnp.exp(jax.random.uniform(keys[0], (M, 1), jnp.float32, math.log(0.5), math.log(2.0)))
    coeff = 0.5 * jax.random.truncated_normal(keys[1], -3.0, 3.0, (M, 8), jnp.float32)
    patterns = jax.random.truncated_normal(keys[2], -4.0, 4.0, (8, CELLS), jnp.float32)
    cell_index = jnp.arange(CELLS, dtype=jnp.int32)
    position = (cell_index % CELL_DEV).astype(jnp.float32) / CELL_DEV
    rough = jnp.exp(jax.random.uniform(keys[3], (1, CELLS), jnp.float32, math.log(0.3), math.log(3.0)))
    noise = jax.random.truncated_normal(keys[4], -4.0, 4.0, (M, CELLS), jnp.float32)
    shared = coeff[:, 0:1] * patterns[0:1]
    for index in range(1, 8):
        shared = shared + coeff[:, index:index + 1] * patterns[index:index + 1]
    ramp = (1.73 * jnp.exp(2.08 * (position - 1.0)))[None, :]
    return (ramp * rough * (spread * noise + shared)).astype(jnp.bfloat16)


def draw_log_weights(key, part):
    values = -200.0 + 1.5 * jax.random.truncated_normal(key, -3.0, 3.0, (M,), jnp.float32)
    return values.astype(jnp.float32)


def setup_inputs(seed: int = 0) -> dict:
    seeds = jax.random.split(jax.random.key(seed), 3)
    ensemble = draw_ensemble(jax.random.fold_in(seeds[2], 71), 0)
    log_weights = draw_log_weights(jax.random.fold_in(seeds[2], 71), 0)
    return {"ensemble": ensemble, "log_weights": log_weights}


def reference(ensemble, log_weights):
    def add_block(total, index):
        piece = lax.dynamic_slice_in_dim(ensemble, index * CELL_DEV, CELL_DEV, 1)
        term = lax.dot_general(piece, piece, (((1,), (1,)), ((), ())), preferred_element_type=jnp.float32)
        return total + term, None

    starts = jnp.arange(N_SPACE, dtype=jnp.int32)
    gram, _ = lax.scan(add_block, jnp.zeros((M, M), jnp.float32), starts)
    norms = jnp.diagonal(gram)
    dist = (norms[:, None] + norms[None, :] - 2.0 * gram) / CELLS
    mean_dist = jnp.sum(dist) / (M * (M - 1))
    kernel = jnp.exp(-dist / (0.08 * mean_dist))
    weights = jax.nn.softmax(log_weights)
    scale_col = jnp.ones((M,), jnp.float32)
    scale_row = weights
    for step in range(ITERS):
        scale_row = weights / jnp.dot(kernel, scale_col, precision=lax.Precision.HIGHEST)
        scale_col = (1.0 / M) / jnp.dot(scale_row, kernel, precision=lax.Precision.HIGHEST)
    coupling = (M * scale_row[:, None] * kernel * scale_col[None, :]).astype(jnp.bfloat16)

    def apply_block(index):
        piece = lax.dynamic_slice_in_dim(ensemble, index * CELL_DEV, CELL_DEV, 1)
        mixed = lax.dot_general(coupling, piece, (((0,), (0,)), ((), ())), preferred_element_type=jnp.float32)
        return mixed.astype(jnp.bfloat16)

    blocks = lax.map(apply_block, starts)
    return jnp.moveaxis(blocks, 0, 1).reshape(M, CELLS)
```

```python
import functools

import jax
import jax.numpy as jnp
from jax import lax
from jax.experimental import pallas as pl
from jax.experimental.pallas import tpu as pltpu
from jax.sharding import Mesh
from jax.sharding import PartitionSpec as P

M = 1024
ITERS = 10
T = 128
NB = M // T
TILES = [(i, j) for i in range(NB) for j in range(i, NB)]
HALF = len(TILES) // 2
ROWS = HALF * T
GROUP = 32
MEM = ("z", "core")
PLANE = ("y", "x")


def eye_mask():
    return lax.broadcasted_iota(jnp.int32, (T, T), 0) == lax.broadcasted_iota(jnp.int32, (T, T), 1)


def distance_kernel(core_ref, relaid_ref, keep_ref, send_ref, packed, sems):
    core = core_ref[0]
    eye = eye_mask()
    norm_row = {}
    for i in reversed(range(NB)):
        rows = relaid_ref[i * T:(i + 1) * T, :]
        strip = lax.dot_general(
            rows, relaid_ref[i * T:, :], (((1,), (1,)), ((), ())), preferred_element_type=jnp.float32
        )
        own = jnp.where(eye, strip[:, :T], 0.0)
        norm_row[i] = jnp.sum(own, axis=0, keepdims=True)
        norm_col = jnp.sum(own, axis=1, keepdims=True)
        for j in range(i, NB):
            tile = TILES.index((i, j))
            half, slot = divmod(tile, HALF)
            gram = strip[:, (j - i) * T:(j - i + 1) * T]
            packed[half, slot * T:(slot + 1) * T, :] = norm_col + norm_row[j] - 2.0 * gram
    keep = pltpu.make_async_copy(packed.at[core], keep_ref, sems.at[0])
    send = pltpu.make_async_copy(packed.at[1 - core], send_ref, sems.at[1])
    send.start()
    keep.start()
    send.wait()
    keep.wait()


def partial_distances(core, relaid):
    shape = jax.ShapeDtypeStruct((ROWS, T), jnp.float32)
    return pl.pallas_call(
        distance_kernel,
        out_shape=(shape, shape),
        grid_spec=pltpu.PrefetchScalarGridSpec(
            num_scalar_prefetch=1,
            grid=(1,),
            in_specs=[pl.BlockSpec(relaid.shape, lambda g, c: (0, 0))],
            out_specs=(pl.BlockSpec(memory_space=pl.ANY), pl.BlockSpec(memory_space=pl.ANY)),
            scratch_shapes=[
                pltpu.VMEM((2, ROWS, T), jnp.float32),
                pltpu.SemaphoreType.DMA((2,)),
            ],
        ),
        compiler_params=pltpu.CompilerParams(vmem_limit_bytes=32 << 20),
        name="distances",
    )(core, relaid)


def analysis_kernel(core_ref, own_ref, other_ref, logw_ref, relaid_ref, out_ref,
                    packed, kern, weight, scale, coup, sems):
    core = core_ref[0]
    first = pltpu.make_async_copy(own_ref, packed.at[core], sems.at[0])
    second = pltpu.make_async_copy(other_ref, packed.at[1 - core], sems.at[1])
    first.start()
    second.start()
    eye = eye_mask()

    def to_column(row):
        return jnp.broadcast_to(jnp.sum(jnp.where(eye, row, 0.0), axis=1, keepdims=True), (T, T))

    logw = logw_ref[...]
    expw = jnp.exp(logw - jnp.max(logw, axis=1, keepdims=True))
    weights = expw / jnp.sum(expw, axis=1, keepdims=True)
    for i in range(NB):
        weight[i * T:(i + 1) * T, :] = to_column(weights[:, i * T:(i + 1) * T])

    first.wait()
    second.wait()

    def tile_of(i, j):
        half, slot = divmod(TILES.index((i, j)), HALF)
        return packed[half, slot * T:(slot + 1) * T, :]

    diagonal = jnp.zeros((8, T), jnp.float32)
    upper = jnp.zeros((8, T), jnp.float32)
    for i, j in TILES:
        part = jnp.sum(tile_of(i, j).reshape(T // 8, 8, T), axis=0)
        if i == j:
            diagonal += part
        else:
            upper += part
    total = jnp.sum(jnp.sum(diagonal + 2.0 * upper, axis=0, keepdims=True), axis=1, keepdims=True)
    mean = total / (M * (M - 1))
    rate = -1.0 / (0.08 * mean)
    for i, j in TILES:
        value = jnp.exp(tile_of(i, j) * rate)
        kern[i * T:(i + 1) * T, j * T:(j + 1) * T] = value
        if i != j:
            kern[j * T:(j + 1) * T, i * T:(i + 1) * T] = value.T

    steps = M // (8 * GROUP)

    def sweep(step, cols):
        wide = [jnp.broadcast_to(c, (8, T)) for c in cols]

        def block(b, sums):
            base = pl.multiple_of(b * (8 * GROUP), 8 * GROUP)
            row_scale = []
            for g in range(GROUP):
                rows = pl.ds(base + 8 * g, 8)
                acc = kern[rows, 0:T] * wide[0]
                for l in range(1, NB):
                    acc += kern[rows, l * T:(l + 1) * T] * wide[l]
                r = weight[rows, :] / jnp.sum(acc, axis=1, keepdims=True)
                scale[rows, :] = r
                row_scale.append(r)
            sums = list(sums)
            for g in range(GROUP):
                rows = pl.ds(base + 8 * g, 8)
                for l in range(NB):
                    sums[l] += kern[rows, l * T:(l + 1) * T] * row_scale[g]
            return tuple(sums)

        zeros = tuple(jnp.zeros((8, T), jnp.float32) for _ in range(NB))
        sums = lax.fori_loop(0, steps, block, zeros)
        return tuple((1.0 / M) / jnp.sum(s, axis=0, keepdims=True) for s in sums)

    ones = tuple(jnp.ones((1, T), jnp.float32) for _ in range(NB))
    cols = lax.fori_loop(0, ITERS, sweep, ones)

    row_scale = [
        M * jnp.sum(jnp.where(eye, scale[i * T:(i + 1) * T, :], 0.0), axis=0, keepdims=True)
        for i in range(NB)
    ]
    for j in range(NB):
        col_scale = to_column(cols[j])
        for i in range(NB):
            value = row_scale[i] * kern[j * T:(j + 1) * T, i * T:(i + 1) * T] * col_scale
            coup[j * T:(j + 1) * T, i * T:(i + 1) * T] = value.astype(jnp.bfloat16)
    for j in range(0, NB, 2):
        mixed = jnp.dot(
            coup[j * T:(j + 2) * T, :], relaid_ref[...], preferred_element_type=jnp.float32
        )
        out_ref[j * T:(j + 2) * T, :] = mixed.astype(jnp.bfloat16)


def analysis_members(core, own, other, log_weights, relaid):
    return pl.pallas_call(
        analysis_kernel,
        out_shape=jax.ShapeDtypeStruct(relaid.shape, jnp.bfloat16),
        grid_spec=pltpu.PrefetchScalarGridSpec(
            num_scalar_prefetch=1,
            grid=(1,),
            in_specs=[
                pl.BlockSpec(memory_space=pl.ANY),
                pl.BlockSpec(memory_space=pl.ANY),
                pl.BlockSpec((1, M), lambda g, c: (0, 0)),
                pl.BlockSpec(relaid.shape, lambda g, c: (0, 0)),
            ],
            out_specs=pl.BlockSpec(relaid.shape, lambda g, c: (0, 0)),
            scratch_shapes=[
                pltpu.VMEM((2, ROWS, T), jnp.float32),
                pltpu.VMEM((M, M), jnp.float32),
                pltpu.VMEM((M, T), jnp.float32),
                pltpu.VMEM((M, T), jnp.float32),
                pltpu.VMEM((M, M), jnp.bfloat16),
                pltpu.SemaphoreType.DMA((2,)),
            ],
        ),
        compiler_params=pltpu.CompilerParams(vmem_limit_bytes=40 << 20),
        name="analysis",
    )(core, own, other, log_weights, relaid)


def per_device(ensemble, log_weights):
    core = lax.axis_index("core").reshape(1)
    plane = lax.axis_size("y") * lax.axis_size("x")
    depth = lax.axis_size("z")
    swap = [(0, 1), (1, 0)]
    relaid = lax.all_to_all(ensemble, MEM, split_axis=1, concat_axis=0, tiled=True)
    keep, send = partial_distances(core, relaid)
    half = keep + lax.ppermute(send, "core", swap)
    parts = lax.all_to_all(half.reshape(plane, ROWS // plane, T), PLANE, 0, 0, tiled=True)
    strip = jnp.sum(parts, axis=0)
    pieces = lax.all_to_all(strip.reshape(depth, -1, T), "z", 0, 0, tiled=True)
    piece = jnp.sum(pieces, axis=0)
    spread = jnp.broadcast_to(piece[None], (depth,) + piece.shape)
    strip = lax.all_to_all(spread, "z", 0, 0, tiled=True).reshape(ROWS // plane, T)
    spread = jnp.broadcast_to(strip[None], (plane,) + strip.shape)
    own = lax.all_to_all(spread, PLANE, 0, 0, tiled=True).reshape(ROWS, T)
    other = lax.ppermute(own, "core", swap)
    mixed = analysis_members(core, own, other, log_weights.reshape(1, M), relaid)
    return lax.all_to_all(mixed, MEM, split_axis=0, concat_axis=1, tiled=True)


def solution(mesh):
    fine = Mesh(mesh.devices.reshape(16, 2, 4, 4), ("z", "core", "y", "x"))
    return jax.shard_map(
        per_device,
        mesh=fine,
        in_specs=(P(MEM, PLANE), P()),
        out_specs=P(MEM, PLANE),
        check_vma=False,
    )
```

```python
import jax
import jax.numpy as jnp
from jax import lax
from jax.experimental import pallas as pl
from jax.experimental.pallas import tpu as pltpu
from jax.sharding import Mesh
from jax.sharding import PartitionSpec as P

M = 1024
ITERS = 10
T = 128
NB = M // T
TILES = [(i, j) for i in range(NB) for j in range(i, NB)]
HALF = len(TILES) // 2
ROWS = HALF * T
HEAD = 8
PLANE_SIZE = 16
DEPTH = 16
STRIP = ROWS // PLANE_SIZE
PIECE = STRIP // DEPTH
PAD = 16
GROUP = 32
MEM = ("z", "core")
PLANE = ("y", "x")


def eye_mask():
    return lax.broadcasted_iota(jnp.int32, (T, T), 0) == lax.broadcasted_iota(jnp.int32, (T, T), 1)


def distance_kernel(core_ref, relaid_ref, keep_ref, send_ref, packed, sems):
    core = core_ref[0]
    eye = eye_mask()
    norm_row = {}
    diagonal = jnp.zeros((8, T), jnp.float32)
    upper = jnp.zeros((8, T), jnp.float32)
    largest = jnp.zeros((8, T), jnp.float32)
    for i in reversed(range(NB)):
        rows = relaid_ref[i * T:(i + 1) * T, :]
        strip = lax.dot_general(
            rows, relaid_ref[i * T:, :], (((1,), (1,)), ((), ())), preferred_element_type=jnp.float32
        )
        own = jnp.where(eye, strip[:, :T], 0.0)
        norm_row[i] = jnp.sum(own, axis=0, keepdims=True)
        norm_col = jnp.sum(own, axis=1, keepdims=True)
        for j in range(i, NB):
            tile = TILES.index((i, j))
            half, slot = divmod(tile, HALF)
            gram = strip[:, (j - i) * T:(j - i + 1) * T]
            value = norm_col + norm_row[j] - 2.0 * gram
            packed[half, slot * T:(slot + 1) * T, :] = value
            folded = value.reshape(T // 8, 8, T)
            largest = jnp.maximum(largest, jnp.max(folded, axis=0))
            if i == j:
                diagonal += jnp.sum(folded, axis=0)
            else:
                upper += jnp.sum(folded, axis=0)
    total = jnp.sum(diagonal + 2.0 * upper, keepdims=True)
    largest = jnp.max(largest, keepdims=True)
    row = lax.broadcasted_iota(jnp.int32, (HEAD, T), 0)
    head = jnp.where(row == 0, total, jnp.where(row == 1, largest, 0.0))
    packed[0, ROWS:, :] = head
    packed[1, ROWS:, :] = head
    keep = pltpu.make_async_copy(packed.at[core], keep_ref, sems.at[0])
    send = pltpu.make_async_copy(packed.at[1 - core], send_ref, sems.at[1])
    send.start()
    keep.start()
    send.wait()
    keep.wait()


def partial_distances(core, relaid):
    shape = jax.ShapeDtypeStruct((ROWS + HEAD, T), jnp.float32)
    return pl.pallas_call(
        distance_kernel,
        out_shape=(shape, shape),
        grid_spec=pltpu.PrefetchScalarGridSpec(
            num_scalar_prefetch=1,
            grid=(1,),
            in_specs=[pl.BlockSpec(relaid.shape, lambda g, c: (0, 0))],
            out_specs=(pl.BlockSpec(memory_space=pl.ANY), pl.BlockSpec(memory_space=pl.ANY)),
            scratch_shapes=[
                pltpu.VMEM((2, ROWS + HEAD, T), jnp.float32),
                pltpu.SemaphoreType.DMA((2,)),
            ],
        ),
        compiler_params=pltpu.CompilerParams(vmem_limit_bytes=32 << 20),
        name="distances",
    )(core, relaid)


def pack_kernel(keep_ref, recv_ref, out_ref):
    head = keep_ref[ROWS:, :] + recv_ref[ROWS:, :]
    bound = jnp.maximum(head[1:2, :], 1e-30)
    power = jnp.floor(15.0 - jnp.log2(bound))
    scale = jnp.exp2(power)
    share = head[0:1, :] * scale * 2.0**-20
    high = share.astype(jnp.bfloat16).astype(jnp.float32)
    middle = (share - high).astype(jnp.bfloat16).astype(jnp.float32)
    low = share - high - middle
    row = lax.broadcasted_iota(jnp.int32, (PAD, T), 0)
    tail = jnp.zeros((PAD, T), jnp.float32)
    for index, value in enumerate((power, high, middle, low)):
        tail = jnp.where(row == index, value, tail)
    for p in range(PLANE_SIZE):
        rows = slice(p * STRIP, (p + 1) * STRIP)
        out_ref[p, :STRIP, :] = (keep_ref[rows, :] + recv_ref[rows, :]) * scale
        out_ref[p, STRIP:, :] = tail


def strip_kernel(parts_ref, out_ref, strip):
    acc = jnp.zeros((STRIP, T), jnp.float32)
    total = jnp.zeros((1, T), jnp.float32)
    for p in range(PLANE_SIZE):
        tail = parts_ref[p, STRIP:, :]
        inverse = jnp.exp2(-tail[0:1, :])
        acc += parts_ref[p, :STRIP, :] * inverse
        total += (tail[1:2, :] + tail[2:3, :] + tail[3:4, :]) * inverse
    strip[:STRIP, :] = acc
    strip[STRIP:, :] = jnp.zeros((PAD, T), jnp.float32)
    row = lax.broadcasted_iota(jnp.int32, (PAD, T), 0)
    total = total * 2.0**20
    for g in range(DEPTH):
        piece = strip[g * PIECE:g * PIECE + PAD, :]
        out_ref[g, :, :] = jnp.where(row == PIECE, total, piece)


def entries_kernel(pieces_ref, out_ref):
    whole = jnp.sum(pieces_ref[...], axis=0)
    mean = whole[PIECE:PIECE + 1, :] / (M * (M - 1))
    entries = jnp.exp(whole * (-1.0 / (0.08 * mean))).astype(jnp.bfloat16)
    for g in range(DEPTH):
        out_ref[g, :, :] = entries


def spread_kernel(pieces_ref, out_ref, strip):
    for g in range(DEPTH):
        strip[g * PIECE:g * PIECE + PAD, :] = pieces_ref[g, :, :].astype(jnp.float32)
    entries = strip[:STRIP, :].astype(jnp.bfloat16)
    for p in range(PLANE_SIZE):
        out_ref[p, :, :] = entries


def small_call(body, shape, dtype, name, scratch=()):
    return pl.pallas_call(
        body,
        out_shape=jax.ShapeDtypeStruct(shape, dtype),
        scratch_shapes=scratch,
        compiler_params=pltpu.CompilerParams(vmem_limit_bytes=16 << 20),
        name=name,
    )


def analysis_kernel(core_ref, own_ref, other_ref, logw_ref, relaid_ref, out_ref,
                    packed, kern, weight, scale, coup, sems):
    core = core_ref[0]
    first = pltpu.make_async_copy(own_ref, packed.at[core], sems.at[0])
    second = pltpu.make_async_copy(other_ref, packed.at[1 - core], sems.at[1])
    first.start()
    second.start()
    eye = eye_mask()

    def to_column(row):
        return jnp.broadcast_to(jnp.sum(jnp.where(eye, row, 0.0), axis=1, keepdims=True), (T, T))

    logw = logw_ref[...]
    expw = jnp.exp(logw - jnp.max(logw, axis=1, keepdims=True))
    weights = expw / jnp.sum(expw, axis=1, keepdims=True)
    for i in range(NB):
        weight[i * T:(i + 1) * T, :] = to_column(weights[:, i * T:(i + 1) * T])

    first.wait()
    second.wait()

    def tile_of(i, j):
        half, slot = divmod(TILES.index((i, j)), HALF)
        return packed[half, slot * T:(slot + 1) * T, :]

    for i, j in TILES:
        value = tile_of(i, j).astype(jnp.float32)
        kern[i * T:(i + 1) * T, j * T:(j + 1) * T] = value
        if i != j:
            kern[j * T:(j + 1) * T, i * T:(i + 1) * T] = value.T

    steps = M // (8 * GROUP)

    def sweep(step, cols):
        wide = [jnp.broadcast_to(c, (8, T)) for c in cols]

        def block(b, sums):
            base = pl.multiple_of(b * (8 * GROUP), 8 * GROUP)
            row_scale = []
            for g in range(GROUP):
                rows = pl.ds(base + 8 * g, 8)
                acc = kern[rows, 0:T] * wide[0]
                for l in range(1, NB):
                    acc += kern[rows, l * T:(l + 1) * T] * wide[l]
                r = weight[rows, :] / jnp.sum(acc, axis=1, keepdims=True)
                scale[rows, :] = r
                row_scale.append(r)
            sums = list(sums)
            for g in range(GROUP):
                rows = pl.ds(base + 8 * g, 8)
                for l in range(NB):
                    sums[l] += kern[rows, l * T:(l + 1) * T] * row_scale[g]
            return tuple(sums)

        zeros = tuple(jnp.zeros((8, T), jnp.float32) for _ in range(NB))
        sums = lax.fori_loop(0, steps, block, zeros)
        return tuple((1.0 / M) / jnp.sum(s, axis=0, keepdims=True) for s in sums)

    ones = tuple(jnp.ones((1, T), jnp.float32) for _ in range(NB))
    cols = lax.fori_loop(0, ITERS, sweep, ones)

    row_scale = [
        M * jnp.sum(jnp.where(eye, scale[i * T:(i + 1) * T, :], 0.0), axis=0, keepdims=True)
        for i in range(NB)
    ]
    for j in range(NB):
        col_scale = to_column(cols[j])
        for i in range(NB):
            value = row_scale[i] * kern[j * T:(j + 1) * T, i * T:(i + 1) * T] * col_scale
            coup[j * T:(j + 1) * T, i * T:(i + 1) * T] = value.astype(jnp.bfloat16)
    for j in range(0, NB, 2):
        mixed = jnp.dot(
            coup[j * T:(j + 2) * T, :], relaid_ref[...], preferred_element_type=jnp.float32
        )
        out_ref[j * T:(j + 2) * T, :] = mixed.astype(jnp.bfloat16)


def analysis_members(core, own, other, log_weights, relaid):
    return pl.pallas_call(
        analysis_kernel,
        out_shape=jax.ShapeDtypeStruct(relaid.shape, jnp.bfloat16),
        grid_spec=pltpu.PrefetchScalarGridSpec(
            num_scalar_prefetch=1,
            grid=(1,),
            in_specs=[
                pl.BlockSpec(memory_space=pl.ANY),
                pl.BlockSpec(memory_space=pl.ANY),
                pl.BlockSpec((1, M), lambda g, c: (0, 0)),
                pl.BlockSpec(relaid.shape, lambda g, c: (0, 0)),
            ],
            out_specs=pl.BlockSpec(relaid.shape, lambda g, c: (0, 0)),
            scratch_shapes=[
                pltpu.VMEM((2, ROWS, T), jnp.bfloat16),
                pltpu.VMEM((M, M), jnp.float32),
                pltpu.VMEM((M, T), jnp.float32),
                pltpu.VMEM((M, T), jnp.float32),
                pltpu.VMEM((M, M), jnp.bfloat16),
                pltpu.SemaphoreType.DMA((2,)),
            ],
        ),
        compiler_params=pltpu.CompilerParams(vmem_limit_bytes=40 << 20),
        name="analysis",
    )(core, own, other, log_weights, relaid)


def per_device(ensemble, log_weights):
    core = lax.axis_index("core").reshape(1)
    swap = [(0, 1), (1, 0)]
    relaid = lax.all_to_all(ensemble, MEM, split_axis=1, concat_axis=0, tiled=True)
    keep, send = partial_distances(core, relaid)
    recv = lax.ppermute(send, "core", swap)
    padded = pltpu.VMEM((STRIP + PAD, T), jnp.float32)
    halves = small_call(pack_kernel, (PLANE_SIZE, STRIP + PAD, T), jnp.float32, "pack")(keep, recv)
    parts = lax.all_to_all(halves.astype(jnp.float16), PLANE, 0, 0, tiled=True).astype(jnp.float32)
    strips = small_call(strip_kernel, (DEPTH, PAD, T), jnp.float32, "strip", [padded])(parts)
    pieces = lax.all_to_all(strips, "z", 0, 0, tiled=True)
    entries = small_call(entries_kernel, (DEPTH, PAD, T), jnp.bfloat16, "entries")(pieces)
    pieces = lax.all_to_all(entries, "z", 0, 0, tiled=True)
    strips = small_call(spread_kernel, (PLANE_SIZE, STRIP, T), jnp.bfloat16, "spread", [padded])(pieces)
    own = lax.all_to_all(strips, PLANE, 0, 0, tiled=True).reshape(ROWS, T)
    other = lax.ppermute(own, "core", swap)
    mixed = analysis_members(core, own, other, log_weights.reshape(1, M), relaid)
    return lax.all_to_all(mixed, MEM, split_axis=0, concat_axis=1, tiled=True)


def solution(mesh):
    fine = Mesh(mesh.devices.reshape(16, 2, 4, 4), ("z", "core", "y", "x"))
    return jax.shard_map(
        per_device,
        mesh=fine,
        in_specs=(P(MEM, PLANE), P()),
        out_specs=P(MEM, PLANE),
        check_vma=False,
    )
```

```python
import jax
import jax.numpy as jnp
from jax import lax
from jax.experimental import pallas as pl
from jax.experimental.pallas import tpu as pltpu
from jax.sharding import Mesh
from jax.sharding import PartitionSpec as P

M = 1024
ITERS = 10
T = 128
NB = M // T
TILES = [(i, j) for i in range(NB) for j in range(i, NB)]
HALF = len(TILES) // 2
ROWS = HALF * T
HEAD = 8
BLOCK_SIZE = 32
BLOCKS = 8
STRIP = ROWS // BLOCK_SIZE
SLAB = STRIP + HEAD
GROUP = 32
MEM = ("zo", "zi", "core")
PLANE = ("y", "x")
BLOCK = ("zi", "y", "x")


def eye_mask():
    return lax.broadcasted_iota(jnp.int32, (T, T), 0) == lax.broadcasted_iota(jnp.int32, (T, T), 1)


def distance_kernel(core_ref, relaid_ref, keep_ref, send_ref, packed, sems):
    core = core_ref[0]
    eye = eye_mask()
    norm_row = {}
    diagonal = jnp.zeros((8, T), jnp.float32)
    upper = jnp.zeros((8, T), jnp.float32)
    largest = jnp.zeros((8, T), jnp.float32)
    for i in reversed(range(NB)):
        rows = relaid_ref[i * T:(i + 1) * T, :]
        strip = lax.dot_general(
            rows, relaid_ref[i * T:, :], (((1,), (1,)), ((), ())), preferred_element_type=jnp.float32
        )
        own = jnp.where(eye, strip[:, :T], 0.0)
        norm_row[i] = jnp.sum(own, axis=0, keepdims=True)
        norm_col = jnp.sum(own, axis=1, keepdims=True)
        for j in range(i, NB):
            tile = TILES.index((i, j))
            half, slot = divmod(tile, HALF)
            gram = strip[:, (j - i) * T:(j - i + 1) * T]
            value = norm_col + norm_row[j] - 2.0 * gram
            packed[half, slot * T:(slot + 1) * T, :] = value
            folded = value.reshape(T // 8, 8, T)
            largest = jnp.maximum(largest, jnp.max(folded, axis=0))
            if i == j:
                diagonal += jnp.sum(folded, axis=0)
            else:
                upper += jnp.sum(folded, axis=0)
    total = jnp.sum(diagonal + 2.0 * upper, keepdims=True)
    largest = jnp.max(largest, keepdims=True)
    row = lax.broadcasted_iota(jnp.int32, (HEAD, T), 0)
    head = jnp.where(row == 0, total, jnp.where(row == 1, largest, 0.0))
    packed[0, ROWS:, :] = head
    packed[1, ROWS:, :] = head
    keep = pltpu.make_async_copy(packed.at[core], keep_ref, sems.at[0])
    send = pltpu.make_async_copy(packed.at[1 - core], send_ref, sems.at[1])
    send.start()
    keep.start()
    send.wait()
    keep.wait()


def partial_distances(core, relaid):
    shape = jax.ShapeDtypeStruct((ROWS + HEAD, T), jnp.float32)
    return pl.pallas_call(
        distance_kernel,
        out_shape=(shape, shape),
        grid_spec=pltpu.PrefetchScalarGridSpec(
            num_scalar_prefetch=1,
            grid=(1,),
            in_specs=[pl.BlockSpec(relaid.shape, lambda g, c: (0, 0))],
            out_specs=(pl.BlockSpec(memory_space=pl.ANY), pl.BlockSpec(memory_space=pl.ANY)),
            scratch_shapes=[
                pltpu.VMEM((2, ROWS + HEAD, T), jnp.float32),
                pltpu.SemaphoreType.DMA((2,)),
            ],
        ),
        compiler_params=pltpu.CompilerParams(vmem_limit_bytes=32 << 20),
        name="distances",
    )(core, relaid)


def scaling(bound):
    power = jnp.floor(15.0 - jnp.log2(jnp.maximum(bound, 1e-30)))
    return power, jnp.exp2(power)


def tail_rows(power, scale, total):
    share = total * scale * 2.0**-20
    high = share.astype(jnp.bfloat16).astype(jnp.float32)
    middle = (share - high).astype(jnp.bfloat16).astype(jnp.float32)
    low = share - high - middle
    row = lax.broadcasted_iota(jnp.int32, (HEAD, T), 0)
    tail = jnp.zeros((HEAD, T), jnp.float32)
    for index, value in enumerate((power, high, middle, low)):
        tail = jnp.where(row == index, value, tail)
    return tail


def summed(parts_ref):
    acc = jnp.zeros((STRIP, T), jnp.float32)
    total = jnp.zeros((1, T), jnp.float32)
    for p in range(parts_ref.shape[0]):
        tail = parts_ref[p, STRIP:, :]
        inverse = jnp.exp2(-tail[0:1, :])
        acc += parts_ref[p, :STRIP, :] * inverse
        total += (tail[1:2, :] + tail[2:3, :] + tail[3:4, :]) * inverse
    return acc, total * 2.0**20


def pack_kernel(keep_ref, recv_ref, out_ref):
    head = keep_ref[ROWS:, :] + recv_ref[ROWS:, :]
    power, scale = scaling(head[1:2, :])
    tail = tail_rows(power, scale, head[0:1, :])
    for p in range(BLOCK_SIZE):
        rows = slice(p * STRIP, (p + 1) * STRIP)
        out_ref[p, :STRIP, :] = (keep_ref[rows, :] + recv_ref[rows, :]) * scale
        out_ref[p, STRIP:, :] = tail


def strip_kernel(parts_ref, out_ref):
    acc, total = summed(parts_ref)
    power, scale = scaling(jnp.maximum(jnp.max(acc, keepdims=True), total * 2.0**-20))
    tail = tail_rows(power, scale, total)
    acc = acc * scale
    for g in range(BLOCKS):
        out_ref[g, :STRIP, :] = acc
        out_ref[g, STRIP:, :] = tail


def entries_kernel(parts_ref, out_ref):
    acc, total = summed(parts_ref)
    mean = total / (M * (M - 1))
    entries = jnp.exp(acc * (-1.0 / (0.08 * mean)))
    entries = jnp.concatenate([entries, jnp.zeros((HEAD, T), jnp.float32)], axis=0)
    entries = entries.astype(jnp.bfloat16)
    for p in range(BLOCK_SIZE):
        out_ref[p, :, :] = entries


def small_call(body, shape, dtype, name):
    return pl.pallas_call(
        body,
        out_shape=jax.ShapeDtypeStruct(shape, dtype),
        compiler_params=pltpu.CompilerParams(vmem_limit_bytes=16 << 20),
        name=name,
    )


def analysis_kernel(core_ref, own_ref, other_ref, logw_ref, relaid_ref, out_ref,
                    packed, kern, weight, scale, coup):
    core = core_ref[0]
    for p in range(BLOCK_SIZE):
        rows = slice(p * STRIP, (p + 1) * STRIP)
        packed[core, rows, :] = own_ref[p].astype(jnp.float32)[:STRIP, :]
        packed[1 - core, rows, :] = other_ref[p].astype(jnp.float32)[:STRIP, :]
    eye = eye_mask()

    def to_column(row):
        return jnp.broadcast_to(jnp.sum(jnp.where(eye, row, 0.0), axis=1, keepdims=True), (T, T))

    logw = logw_ref[...]
    expw = jnp.exp(logw - jnp.max(logw, axis=1, keepdims=True))
    weights = expw / jnp.sum(expw, axis=1, keepdims=True)
    for i in range(NB):
        weight[i * T:(i + 1) * T, :] = to_column(weights[:, i * T:(i + 1) * T])

    def tile_of(i, j):
        half, slot = divmod(TILES.index((i, j)), HALF)
        return packed[half, slot * T:(slot + 1) * T, :]

    for i, j in TILES:
        value = tile_of(i, j)
        kern[i * T:(i + 1) * T, j * T:(j + 1) * T] = value
        if i != j:
            kern[j * T:(j + 1) * T, i * T:(i + 1) * T] = value.T

    steps = M // (8 * GROUP)

    def sweep(step, cols):
        wide = [jnp.broadcast_to(c, (8, T)) for c in cols]

        def block(b, sums):
            base = pl.multiple_of(b * (8 * GROUP), 8 * GROUP)
            row_scale = []
            for g in range(GROUP):
                rows = pl.ds(base + 8 * g, 8)
                acc = kern[rows, 0:T] * wide[0]
                for l in range(1, NB):
                    acc += kern[rows, l * T:(l + 1) * T] * wide[l]
                r = weight[rows, :] / jnp.sum(acc, axis=1, keepdims=True)
                scale[rows, :] = r
                row_scale.append(r)
            sums = list(sums)
            for g in range(GROUP):
                rows = pl.ds(base + 8 * g, 8)
                for l in range(NB):
                    sums[l] += kern[rows, l * T:(l + 1) * T] * row_scale[g]
            return tuple(sums)

        zeros = tuple(jnp.zeros((8, T), jnp.float32) for _ in range(NB))
        sums = lax.fori_loop(0, steps, block, zeros)
        return tuple((1.0 / M) / jnp.sum(s, axis=0, keepdims=True) for s in sums)

    ones = tuple(jnp.ones((1, T), jnp.float32) for _ in range(NB))
    cols = lax.fori_loop(0, ITERS, sweep, ones)

    row_scale = [
        M * jnp.sum(jnp.where(eye, scale[i * T:(i + 1) * T, :], 0.0), axis=0, keepdims=True)
        for i in range(NB)
    ]
    for j in range(NB):
        col_scale = to_column(cols[j])
        for i in range(NB):
            value = row_scale[i] * kern[j * T:(j + 1) * T, i * T:(i + 1) * T] * col_scale
            coup[j * T:(j + 1) * T, i * T:(i + 1) * T] = value.astype(jnp.bfloat16)
    for j in range(0, NB, 2):
        mixed = jnp.dot(
            coup[j * T:(j + 2) * T, :], relaid_ref[...], preferred_element_type=jnp.float32
        )
        out_ref[j * T:(j + 2) * T, :] = mixed.astype(jnp.bfloat16)


def analysis_members(core, own, other, log_weights, relaid):
    vmem = pl.BlockSpec(memory_space=pltpu.VMEM)
    return pl.pallas_call(
        analysis_kernel,
        out_shape=jax.ShapeDtypeStruct(relaid.shape, jnp.bfloat16),
        in_specs=[pl.BlockSpec(memory_space=pltpu.SMEM), vmem, vmem, vmem, vmem],
        out_specs=vmem,
        scratch_shapes=[
            pltpu.VMEM((2, ROWS, T), jnp.float32),
            pltpu.VMEM((M, M), jnp.float32),
            pltpu.VMEM((M, T), jnp.float32),
            pltpu.VMEM((M, T), jnp.float32),
            pltpu.VMEM((M, M), jnp.bfloat16),
        ],
        compiler_params=pltpu.CompilerParams(vmem_limit_bytes=40 << 20),
        name="analysis",
    )(core, own, other, log_weights, relaid)


def exchange(values, axes):
    return lax.all_to_all(values, axes, 0, 0, tiled=True)


def per_device(ensemble, log_weights):
    core = lax.axis_index("core").reshape(1)
    swap = [(0, 1), (1, 0)]
    relaid = lax.all_to_all(ensemble, MEM, split_axis=1, concat_axis=0, tiled=True)
    keep, send = partial_distances(core, relaid)
    recv = lax.ppermute(send, "core", swap)
    slabs = small_call(pack_kernel, (BLOCK_SIZE, SLAB, T), jnp.float32, "pack")(keep, recv)
    parts = exchange(slabs.astype(jnp.float16), BLOCK).astype(jnp.float32)
    strips = small_call(strip_kernel, (BLOCKS, SLAB, T), jnp.float32, "strip")(parts)
    parts = exchange(strips.astype(jnp.float16), "zo").astype(jnp.float32)
    entries = small_call(entries_kernel, (BLOCK_SIZE, SLAB, T), jnp.bfloat16, "entries")(parts)
    own = exchange(entries, BLOCK)
    other = lax.ppermute(own, "core", swap)
    mixed = analysis_members(core, own, other, log_weights.reshape(1, M), relaid)
    return lax.all_to_all(mixed, MEM, split_axis=0, concat_axis=1, tiled=True)


def solution(mesh):
    fine = Mesh(mesh.devices.reshape(8, 2, 2, 4, 4), ("zo", "zi", "core", "y", "x"))
    return jax.shard_map(
        per_device,
        mesh=fine,
        in_specs=(P(MEM, PLANE), P()),
        out_specs=P(MEM, PLANE),
        check_vma=False,
    )
```

```python
import jax
import jax.numpy as jnp
from jax import lax
from jax.experimental import pallas as pl
from jax.experimental.pallas import tpu as pltpu
from jax.sharding import Mesh
from jax.sharding import PartitionSpec as P

M = 1024
ITERS = 10
T = 128
NB = M // T
TILES = [(i, j) for i in range(NB) for j in range(i, NB)]
HALF = len(TILES) // 2
ROWS = HALF * T
HEAD = 8
BLOCK_SIZE = 32
BLOCKS = 8
STRIP = ROWS // BLOCK_SIZE
SLAB = STRIP + HEAD
SPLIT = 512
GROUP = 16
MEM = ("zo", "zi", "core")
PLANE = ("y", "x")
BLOCK = ("zi", "y", "x")


def eye_mask():
    return lax.broadcasted_iota(jnp.int32, (T, T), 0) == lax.broadcasted_iota(jnp.int32, (T, T), 1)


def split_kernel(ensemble_ref, out_ref):
    count, _, cells = out_ref.shape
    for d in range(count):
        out_ref[d] = ensemble_ref[:, d * cells:(d + 1) * cells]


def join_kernel(blocks_ref, out_ref, sems):
    count, _, cells = blocks_ref.shape
    copies = [
        pltpu.make_async_copy(blocks_ref.at[d], out_ref.at[:, d * cells:(d + 1) * cells], sems.at[d])
        for d in range(count)
    ]
    for copy in copies:
        copy.start()
    for copy in copies:
        copy.wait()


def split_cells(ensemble, shape):
    return pl.pallas_call(
        split_kernel,
        out_shape=jax.ShapeDtypeStruct(shape, ensemble.dtype),
        in_specs=[pl.BlockSpec(memory_space=pltpu.VMEM)],
        out_specs=pl.BlockSpec(memory_space=pltpu.VMEM),
        compiler_params=pltpu.CompilerParams(vmem_limit_bytes=8 << 20),
        name="split",
    )(ensemble)


def join_cells(blocks, shape):
    return pl.pallas_call(
        join_kernel,
        out_shape=jax.ShapeDtypeStruct(shape, blocks.dtype),
        in_specs=[pl.BlockSpec(memory_space=pltpu.VMEM)],
        out_specs=pl.BlockSpec(memory_space=pltpu.HBM),
        scratch_shapes=[pltpu.SemaphoreType.DMA((blocks.shape[0],))],
        compiler_params=pltpu.CompilerParams(vmem_limit_bytes=8 << 20),
        name="join",
    )(blocks)


def distance_kernel(relaid_ref, keep_ref, send_ref, packed):
    core = lax.axis_index("core")
    eye = eye_mask()
    norm_row = {}
    diagonal = jnp.zeros((8, T), jnp.float32)
    upper = jnp.zeros((8, T), jnp.float32)
    largest = jnp.zeros((8, T), jnp.float32)
    for i in reversed(range(NB)):
        rows = relaid_ref[i * T:(i + 1) * T, :]
        strip = lax.dot_general(
            rows, relaid_ref[i * T:, :], (((1,), (1,)), ((), ())), preferred_element_type=jnp.float32
        )
        own = jnp.where(eye, strip[:, :T], 0.0)
        norm_row[i] = jnp.sum(own, axis=0, keepdims=True)
        norm_col = jnp.sum(own, axis=1, keepdims=True)
        for j in range(i, NB):
            tile = TILES.index((i, j))
            half, slot = divmod(tile, HALF)
            gram = strip[:, (j - i) * T:(j - i + 1) * T]
            value = norm_col + norm_row[j] - 2.0 * gram
            packed[half, slot * T:(slot + 1) * T, :] = value
            folded = value.reshape(T // 8, 8, T)
            largest = jnp.maximum(largest, jnp.max(folded, axis=0))
            if i == j:
                diagonal += jnp.sum(folded, axis=0)
            else:
                upper += jnp.sum(folded, axis=0)
    total = jnp.sum(diagonal + 2.0 * upper, keepdims=True)
    largest = jnp.max(largest, keepdims=True)
    row = lax.broadcasted_iota(jnp.int32, (HEAD, T), 0)
    head = jnp.where(row == 0, total, jnp.where(row == 1, largest, 0.0))
    packed[0, ROWS:, :] = head
    packed[1, ROWS:, :] = head
    keep_ref[...] = packed[core]
    send_ref[...] = packed[1 - core]


def partial_distances(relaid):
    shape = jax.ShapeDtypeStruct((ROWS + HEAD, T), jnp.float32)
    vmem = pl.BlockSpec(memory_space=pltpu.VMEM)
    return pl.pallas_call(
        distance_kernel,
        out_shape=(shape, shape),
        in_specs=[vmem],
        out_specs=(vmem, vmem),
        scratch_shapes=[pltpu.VMEM((2, ROWS + HEAD, T), jnp.float32)],
        compiler_params=pltpu.CompilerParams(vmem_limit_bytes=32 << 20),
        name="distances",
    )(relaid)


def scaling(bound):
    power = jnp.floor(15.0 - jnp.log2(jnp.maximum(bound, 1e-30)))
    return power, jnp.exp2(power)


def tail_rows(power, scale, total):
    share = total * scale * 2.0**-20
    high = share.astype(jnp.bfloat16).astype(jnp.float32)
    middle = (share - high).astype(jnp.bfloat16).astype(jnp.float32)
    low = share - high - middle
    row = lax.broadcasted_iota(jnp.int32, (HEAD, T), 0)
    tail = jnp.zeros((HEAD, T), jnp.float32)
    for index, value in enumerate((power, high, middle, low)):
        tail = jnp.where(row == index, value, tail)
    return tail


def summed(parts_ref):
    acc = jnp.zeros((STRIP, T), jnp.float32)
    total = jnp.zeros((1, T), jnp.float32)
    for p in range(parts_ref.shape[0]):
        tail = parts_ref[p, STRIP:, :]
        inverse = jnp.exp2(-tail[0:1, :])
        acc += parts_ref[p, :STRIP, :] * inverse
        total += (tail[1:2, :] + tail[2:3, :] + tail[3:4, :]) * inverse
    return acc, total * 2.0**20


def pack_kernel(keep_ref, recv_ref, out_ref):
    head = keep_ref[ROWS:, :] + recv_ref[ROWS:, :]
    power, scale = scaling(head[1:2, :])
    tail = tail_rows(power, scale, head[0:1, :])
    for p in range(BLOCK_SIZE):
        rows = slice(p * STRIP, (p + 1) * STRIP)
        out_ref[p, :STRIP, :] = (keep_ref[rows, :] + recv_ref[rows, :]) * scale
        out_ref[p, STRIP:, :] = tail


def strip_kernel(parts_ref, out_ref):
    acc, total = summed(parts_ref)
    power, scale = scaling(jnp.maximum(jnp.max(acc, keepdims=True), total * 2.0**-20))
    tail = tail_rows(power, scale, total)
    acc = acc * scale
    for g in range(BLOCKS):
        out_ref[g, :STRIP, :] = acc
        out_ref[g, STRIP:, :] = tail


def entries_kernel(parts_ref, out_ref):
    acc, total = summed(parts_ref)
    mean = total / (M * (M - 1))
    entries = jnp.exp(acc * (-1.0 / (0.08 * mean)))
    entries = jnp.concatenate([entries, jnp.zeros((HEAD, T), jnp.float32)], axis=0)
    entries = entries.astype(jnp.bfloat16)
    for p in range(BLOCK_SIZE):
        out_ref[p, :, :] = entries


def small_call(body, shape, dtype, name):
    return pl.pallas_call(
        body,
        out_shape=jax.ShapeDtypeStruct(shape, dtype),
        compiler_params=pltpu.CompilerParams(vmem_limit_bytes=16 << 20),
        name=name,
    )


def analysis_kernel(own_ref, other_ref, logw_ref, relaid_ref, out_ref,
                    packed, kern_a, kern_at, kern_b, weight, scale, coup):
    core = lax.axis_index("core")
    for p in range(BLOCK_SIZE):
        rows = slice(p * STRIP, (p + 1) * STRIP)
        packed[core, rows, :] = own_ref[p].astype(jnp.float32)[:STRIP, :]
        packed[1 - core, rows, :] = other_ref[p].astype(jnp.float32)[:STRIP, :]

    def place(i, j, value):
        cols = slice(j * T, (j + 1) * T)
        if i * T < SPLIT:
            kern_a[i * T:(i + 1) * T, cols] = value.astype(jnp.bfloat16)
        else:
            kern_b[i * T - SPLIT:(i + 1) * T - SPLIT, cols] = value
        if j * T < SPLIT:
            kern_at[i * T:(i + 1) * T, cols] = value.astype(jnp.bfloat16)

    for tile, (i, j) in enumerate(TILES):
        half, slot = divmod(tile, HALF)
        value = packed[half, slot * T:(slot + 1) * T, :]
        place(i, j, value)
        if i != j:
            place(j, i, value.T)

    eye = eye_mask()

    def to_column(row):
        return jnp.broadcast_to(jnp.sum(jnp.where(eye, row, 0.0), axis=1, keepdims=True), (T, T))

    logw = logw_ref[...]
    expw = jnp.exp(logw - jnp.max(logw, axis=1, keepdims=True))
    weights = expw / jnp.sum(expw, axis=1, keepdims=True)
    for i in range(SPLIT // T, NB):
        weight[i * T - SPLIT:(i + 1) * T - SPLIT, :] = to_column(weights[:, i * T:(i + 1) * T])

    def product(vector, matrix):
        first = vector.astype(jnp.bfloat16).astype(jnp.float32)
        second = (vector - first).astype(jnp.bfloat16).astype(jnp.float32)
        third = vector - first - second
        row = lax.broadcasted_iota(jnp.int32, (16, vector.shape[1]), 0)
        parts = jnp.where(row == 0, first, jnp.where(row == 1, second, jnp.where(row == 2, third, 0.0)))
        sums = jnp.dot(parts.astype(jnp.bfloat16), matrix, preferred_element_type=jnp.float32)
        return sums[0:1, :] + sums[1:2, :] + sums[2:3, :]

    def sweep(step, scales):
        scale_col = scales[1]
        scale_a = weights[:, :SPLIT] / product(scale_col, kern_at[...])
        from_a = product(scale_a, kern_a[...])
        wide = [jnp.broadcast_to(scale_col[:, l * T:(l + 1) * T], (8, T)) for l in range(NB)]
        sums = [jnp.zeros((8, T), jnp.float32) for _ in range(NB)]
        for base in range(0, M - SPLIT, 8 * GROUP):
            row_scale = []
            for g in range(GROUP):
                rows = slice(base + 8 * g, base + 8 * g + 8)
                acc = kern_b[rows, 0:T] * wide[0]
                for l in range(1, NB):
                    acc += kern_b[rows, l * T:(l + 1) * T] * wide[l]
                r = weight[rows, :] / jnp.sum(acc, axis=1, keepdims=True)
                scale[rows, :] = r
                row_scale.append(r)
            for g in range(GROUP):
                rows = slice(base + 8 * g, base + 8 * g + 8)
                for l in range(NB):
                    sums[l] += kern_b[rows, l * T:(l + 1) * T] * row_scale[g]
        from_b = jnp.concatenate([jnp.sum(s, axis=0, keepdims=True) for s in sums], axis=1)
        return scale_a, (1.0 / M) / (from_a + from_b)

    start = (weights[:, :SPLIT], jnp.ones((1, M), jnp.float32))
    scale_a, scale_col = lax.fori_loop(0, ITERS, sweep, start)

    scale_row = [M * scale_a[:, i * T:(i + 1) * T] for i in range(SPLIT // T)]
    for i in range(SPLIT // T, NB):
        block = scale[i * T - SPLIT:(i + 1) * T - SPLIT, :]
        scale_row.append(M * jnp.sum(jnp.where(eye, block, 0.0), axis=0, keepdims=True))
    for j in range(NB):
        rows = slice(j * T, (j + 1) * T)
        column = to_column(scale_col[:, rows])
        for i in range(NB):
            cols = slice(i * T, (i + 1) * T)
            if j * T < SPLIT:
                value = kern_a[rows, cols].astype(jnp.float32)
            else:
                value = kern_b[j * T - SPLIT:(j + 1) * T - SPLIT, cols]
            coup[rows, cols] = (scale_row[i] * value * column).astype(jnp.bfloat16)
    for j in range(0, NB, 2):
        mixed = jnp.dot(
            coup[j * T:(j + 2) * T, :], relaid_ref[...], preferred_element_type=jnp.float32
        )
        out_ref[j * T:(j + 2) * T, :] = mixed.astype(jnp.bfloat16)


def analysis_members(own, other, log_weights, relaid):
    vmem = pl.BlockSpec(memory_space=pltpu.VMEM)
    return pl.pallas_call(
        analysis_kernel,
        out_shape=jax.ShapeDtypeStruct(relaid.shape, jnp.bfloat16),
        in_specs=[vmem, vmem, vmem, vmem],
        out_specs=vmem,
        scratch_shapes=[
            pltpu.VMEM((2, ROWS, T), jnp.float32),
            pltpu.VMEM((SPLIT, M), jnp.bfloat16),
            pltpu.VMEM((M, SPLIT), jnp.bfloat16),
            pltpu.VMEM((M - SPLIT, M), jnp.float32),
            pltpu.VMEM((M - SPLIT, T), jnp.float32),
            pltpu.VMEM((M - SPLIT, T), jnp.float32),
            pltpu.VMEM((M, M), jnp.bfloat16),
        ],
        compiler_params=pltpu.CompilerParams(vmem_limit_bytes=40 << 20),
        name="analysis",
    )(own, other, log_weights, relaid)


def exchange(values, axes):
    return lax.all_to_all(values, axes, 0, 0, tiled=True)


def per_device(ensemble, log_weights):
    swap = [(0, 1), (1, 0)]
    rows, cells = ensemble.shape
    count = M // rows
    shape = (count, rows, cells // count)
    blocks = split_cells(ensemble, shape)
    relaid = exchange(blocks, MEM).reshape(M, cells // count)
    keep, send = partial_distances(relaid)
    recv = lax.ppermute(send, "core", swap)
    slabs = small_call(pack_kernel, (BLOCK_SIZE, SLAB, T), jnp.float32, "pack")(keep, recv)
    parts = exchange(slabs.astype(jnp.float16), BLOCK).astype(jnp.float32)
    strips = small_call(strip_kernel, (BLOCKS, SLAB, T), jnp.float32, "strip")(parts)
    parts = exchange(strips.astype(jnp.float16), "zo").astype(jnp.float32)
    entries = small_call(entries_kernel, (BLOCK_SIZE, SLAB, T), jnp.bfloat16, "entries")(parts)
    own = exchange(entries, BLOCK)
    other = lax.ppermute(own, "core", swap)
    mixed = analysis_members(own, other, log_weights.reshape(1, M), relaid)
    blocks = exchange(mixed.reshape(shape), MEM)
    return join_cells(blocks, ensemble.shape)


def solution(mesh):
    fine = Mesh(mesh.devices.reshape(8, 2, 2, 4, 4), ("zo", "zi", "core", "y", "x"))
    return jax.shard_map(
        per_device,
        mesh=fine,
        in_specs=(P(MEM, PLANE), P()),
        out_specs=P(MEM, PLANE),
        check_vma=False,
    )
```

```python
import jax
import jax.numpy as jnp
from jax import lax
from jax.experimental import pallas as pl
from jax.experimental.pallas import tpu as pltpu
from jax.sharding import Mesh
from jax.sharding import PartitionSpec as P

M = 1024
OWN = 32
ITERS = 10
T = 128
NB = M // T
TILES = [(i, j) for i in range(NB) for j in range(i, NB)]
HALF = len(TILES) // 2
ROWS = HALF * T
HEAD = 8
BLOCK_SIZE = 32
BLOCKS = 8
STRIP = ROWS // BLOCK_SIZE
SLAB = STRIP + HEAD
SPLIT = 512
GROUP = 16
MEM = ("zo", "zi", "core")
PLANE = ("y", "x")
BLOCK = ("zi", "y", "x")


def eye_mask():
    return lax.broadcasted_iota(jnp.int32, (T, T), 0) == lax.broadcasted_iota(jnp.int32, (T, T), 1)


def split_kernel(ensemble_ref, out_ref):
    count, _, cells = out_ref.shape
    for d in range(count):
        out_ref[d] = ensemble_ref[:, d * cells:(d + 1) * cells]


def join_kernel(blocks_ref, out_ref, sems):
    count, _, cells = blocks_ref.shape
    copies = [
        pltpu.make_async_copy(blocks_ref.at[d], out_ref.at[:, d * cells:(d + 1) * cells], sems.at[d])
        for d in range(count)
    ]
    for copy in copies:
        copy.start()
    for copy in copies:
        copy.wait()


def split_cells(ensemble, shape):
    return pl.pallas_call(
        split_kernel,
        out_shape=jax.ShapeDtypeStruct(shape, ensemble.dtype),
        in_specs=[pl.BlockSpec(memory_space=pltpu.VMEM)],
        out_specs=pl.BlockSpec(memory_space=pltpu.VMEM),
        compiler_params=pltpu.CompilerParams(vmem_limit_bytes=8 << 20),
        name="split",
    )(ensemble)


def join_cells(blocks, shape):
    return pl.pallas_call(
        join_kernel,
        out_shape=jax.ShapeDtypeStruct(shape, blocks.dtype),
        in_specs=[pl.BlockSpec(memory_space=pltpu.VMEM)],
        out_specs=pl.BlockSpec(memory_space=pltpu.HBM),
        scratch_shapes=[pltpu.SemaphoreType.DMA((blocks.shape[0],))],
        compiler_params=pltpu.CompilerParams(vmem_limit_bytes=8 << 20),
        name="join",
    )(blocks)


def distance_kernel(relaid_ref, keep_ref, send_ref, packed):
    core = lax.axis_index("core")
    eye = eye_mask()
    norm_row = {}
    diagonal = jnp.zeros((8, T), jnp.float32)
    upper = jnp.zeros((8, T), jnp.float32)
    largest = jnp.zeros((8, T), jnp.float32)
    for i in reversed(range(NB)):
        rows = relaid_ref[i * T:(i + 1) * T, :]
        strip = lax.dot_general(
            rows, relaid_ref[i * T:, :], (((1,), (1,)), ((), ())), preferred_element_type=jnp.float32
        )
        own = jnp.where(eye, strip[:, :T], 0.0)
        norm_row[i] = jnp.sum(own, axis=0, keepdims=True)
        norm_col = jnp.sum(own, axis=1, keepdims=True)
        for j in range(i, NB):
            tile = TILES.index((i, j))
            half, slot = divmod(tile, HALF)
            gram = strip[:, (j - i) * T:(j - i + 1) * T]
            value = norm_col + norm_row[j] - 2.0 * gram
            packed[half, slot * T:(slot + 1) * T, :] = value
            folded = value.reshape(T // 8, 8, T)
            largest = jnp.maximum(largest, jnp.max(folded, axis=0))
            if i == j:
                diagonal += jnp.sum(folded, axis=0)
            else:
                upper += jnp.sum(folded, axis=0)
    total = jnp.sum(diagonal + 2.0 * upper, keepdims=True)
    largest = jnp.max(largest, keepdims=True)
    row = lax.broadcasted_iota(jnp.int32, (HEAD, T), 0)
    head = jnp.where(row == 0, total, jnp.where(row == 1, largest, 0.0))
    packed[0, ROWS:, :] = head
    packed[1, ROWS:, :] = head
    keep_ref[...] = packed[core]
    send_ref[...] = packed[1 - core]


def partial_distances(relaid):
    shape = jax.ShapeDtypeStruct((ROWS + HEAD, T), jnp.float32)
    vmem = pl.BlockSpec(memory_space=pltpu.VMEM)
    return pl.pallas_call(
        distance_kernel,
        out_shape=(shape, shape),
        in_specs=[vmem],
        out_specs=(vmem, vmem),
        scratch_shapes=[pltpu.VMEM((2, ROWS + HEAD, T), jnp.float32)],
        compiler_params=pltpu.CompilerParams(vmem_limit_bytes=32 << 20),
        name="distances",
    )(relaid)


def scaling(bound):
    power = jnp.floor(15.0 - jnp.log2(jnp.maximum(bound, 1e-30)))
    return power, jnp.exp2(power)


def tail_rows(power, scale, total):
    share = total * scale * 2.0**-20
    high = share.astype(jnp.bfloat16).astype(jnp.float32)
    middle = (share - high).astype(jnp.bfloat16).astype(jnp.float32)
    low = share - high - middle
    row = lax.broadcasted_iota(jnp.int32, (HEAD, T), 0)
    tail = jnp.zeros((HEAD, T), jnp.float32)
    for index, value in enumerate((power, high, middle, low)):
        tail = jnp.where(row == index, value, tail)
    return tail


def summed(parts_ref):
    acc = jnp.zeros((STRIP, T), jnp.float32)
    total = jnp.zeros((1, T), jnp.float32)
    for p in range(parts_ref.shape[0]):
        tail = parts_ref[p, STRIP:, :]
        inverse = jnp.exp2(-tail[0:1, :])
        acc += parts_ref[p, :STRIP, :] * inverse
        total += (tail[1:2, :] + tail[2:3, :] + tail[3:4, :]) * inverse
    return acc, total * 2.0**20


def pack_kernel(keep_ref, recv_ref, out_ref):
    head = keep_ref[ROWS:, :] + recv_ref[ROWS:, :]
    power, scale = scaling(head[1:2, :])
    tail = tail_rows(power, scale, head[0:1, :])
    for p in range(BLOCK_SIZE):
        rows = slice(p * STRIP, (p + 1) * STRIP)
        out_ref[p, :STRIP, :] = (keep_ref[rows, :] + recv_ref[rows, :]) * scale
        out_ref[p, STRIP:, :] = tail


def strip_kernel(parts_ref, out_ref):
    acc, total = summed(parts_ref)
    power, scale = scaling(jnp.maximum(jnp.max(acc, keepdims=True), total * 2.0**-20))
    tail = tail_rows(power, scale, total)
    acc = acc * scale
    for g in range(BLOCKS):
        out_ref[g, :STRIP, :] = acc
        out_ref[g, STRIP:, :] = tail


def entries_kernel(parts_ref, out_ref):
    acc, total = summed(parts_ref)
    mean = total / (M * (M - 1))
    entries = jnp.exp(acc * (-1.0 / (0.08 * mean)))
    entries = jnp.concatenate([entries, jnp.zeros((HEAD, T), jnp.float32)], axis=0)
    entries = entries.astype(jnp.bfloat16)
    for p in range(BLOCK_SIZE):
        out_ref[p, :, :] = entries


def small_call(body, shape, dtype, name):
    return pl.pallas_call(
        body,
        out_shape=jax.ShapeDtypeStruct(shape, dtype),
        compiler_params=pltpu.CompilerParams(vmem_limit_bytes=16 << 20),
        name=name,
    )


def analysis_kernel(own_ref, other_ref, logw_ref, relaid_ref, out_ref,
                    packed, kern_a, kern_at, kern_b, weight, scale, coup):
    core = lax.axis_index("core")
    for p in range(BLOCK_SIZE):
        rows = slice(p * STRIP, (p + 1) * STRIP)
        packed[core, rows, :] = own_ref[p].astype(jnp.float32)[:STRIP, :]
        packed[1 - core, rows, :] = other_ref[p].astype(jnp.float32)[:STRIP, :]

    def place(i, j, value):
        cols = slice(j * T, (j + 1) * T)
        if i * T < SPLIT:
            kern_a[i * T:(i + 1) * T, cols] = value.astype(jnp.bfloat16)
        else:
            kern_b[i * T - SPLIT:(i + 1) * T - SPLIT, cols] = value
        if j * T < SPLIT:
            kern_at[i * T:(i + 1) * T, cols] = value.astype(jnp.bfloat16)

    for tile, (i, j) in enumerate(TILES):
        half, slot = divmod(tile, HALF)
        value = packed[half, slot * T:(slot + 1) * T, :]
        place(i, j, value)
        if i != j:
            place(j, i, value.T)

    eye = eye_mask()

    def to_column(row):
        return jnp.broadcast_to(jnp.sum(jnp.where(eye, row, 0.0), axis=1, keepdims=True), (T, T))

    logw = logw_ref[...]
    expw = jnp.exp(logw - jnp.max(logw, axis=1, keepdims=True))
    weights = expw / jnp.sum(expw, axis=1, keepdims=True)
    weights = jnp.concatenate(
        [weights[:, k * OWN:(k + 1) * OWN] for k in reversed(range(M // OWN))], axis=1
    )
    for i in range(SPLIT // T, NB):
        weight[i * T - SPLIT:(i + 1) * T - SPLIT, :] = to_column(weights[:, i * T:(i + 1) * T])

    def product(vector, matrix):
        first = vector.astype(jnp.bfloat16).astype(jnp.float32)
        second = (vector - first).astype(jnp.bfloat16).astype(jnp.float32)
        third = vector - first - second
        row = lax.broadcasted_iota(jnp.int32, (16, vector.shape[1]), 0)
        parts = jnp.where(row == 0, first, jnp.where(row == 1, second, jnp.where(row == 2, third, 0.0)))
        sums = jnp.dot(parts.astype(jnp.bfloat16), matrix, preferred_element_type=jnp.float32)
        return sums[0:1, :] + sums[1:2, :] + sums[2:3, :]

    def sweep(step, scales):
        scale_col = scales[1]
        scale_a = weights[:, :SPLIT] / product(scale_col, kern_at[...])
        from_a = product(scale_a, kern_a[...])
        wide = [jnp.broadcast_to(scale_col[:, l * T:(l + 1) * T], (8, T)) for l in range(NB)]
        sums = [jnp.zeros((8, T), jnp.float32) for _ in range(NB)]
        for base in range(0, M - SPLIT, 8 * GROUP):
            row_scale = []
            for g in range(GROUP):
                rows = slice(base + 8 * g, base + 8 * g + 8)
                acc = kern_b[rows, 0:T] * wide[0]
                for l in range(1, NB):
                    acc += kern_b[rows, l * T:(l + 1) * T] * wide[l]
                r = weight[rows, :] / jnp.sum(acc, axis=1, keepdims=True)
                scale[rows, :] = r
                row_scale.append(r)
            for g in range(GROUP):
                rows = slice(base + 8 * g, base + 8 * g + 8)
                for l in range(NB):
                    sums[l] += kern_b[rows, l * T:(l + 1) * T] * row_scale[g]
        from_b = jnp.concatenate([jnp.sum(s, axis=0, keepdims=True) for s in sums], axis=1)
        return scale_a, (1.0 / M) / (from_a + from_b)

    start = (weights[:, :SPLIT], jnp.ones((1, M), jnp.float32))
    scale_a, scale_col = lax.fori_loop(0, ITERS, sweep, start)

    scale_row = [M * scale_a[:, i * T:(i + 1) * T] for i in range(SPLIT // T)]
    for i in range(SPLIT // T, NB):
        block = scale[i * T - SPLIT:(i + 1) * T - SPLIT, :]
        scale_row.append(M * jnp.sum(jnp.where(eye, block, 0.0), axis=0, keepdims=True))
    for j in range(NB):
        rows = slice(j * T, (j + 1) * T)
        column = to_column(scale_col[:, rows])
        for i in range(NB):
            cols = slice(i * T, (i + 1) * T)
            if j * T < SPLIT:
                value = kern_a[rows, cols].astype(jnp.float32)
            else:
                value = kern_b[j * T - SPLIT:(j + 1) * T - SPLIT, cols]
            coup[rows, cols] = (scale_row[i] * value * column).astype(jnp.bfloat16)
    for j in range(0, NB, 2):
        mixed = jnp.dot(
            coup[j * T:(j + 2) * T, :], relaid_ref[...], preferred_element_type=jnp.float32
        )
        out_ref[j * T:(j + 2) * T, :] = mixed.astype(jnp.bfloat16)


def analysis_members(own, other, log_weights, relaid):
    vmem = pl.BlockSpec(memory_space=pltpu.VMEM)
    return pl.pallas_call(
        analysis_kernel,
        out_shape=jax.ShapeDtypeStruct(relaid.shape, jnp.bfloat16),
        in_specs=[vmem, vmem, vmem, vmem],
        out_specs=vmem,
        scratch_shapes=[
            pltpu.VMEM((2, ROWS, T), jnp.float32),
            pltpu.VMEM((SPLIT, M), jnp.bfloat16),
            pltpu.VMEM((M, SPLIT), jnp.bfloat16),
            pltpu.VMEM((M - SPLIT, M), jnp.float32),
            pltpu.VMEM((M - SPLIT, T), jnp.float32),
            pltpu.VMEM((M - SPLIT, T), jnp.float32),
            pltpu.VMEM((M, M), jnp.bfloat16),
        ],
        compiler_params=pltpu.CompilerParams(vmem_limit_bytes=40 << 20),
        name="analysis",
    )(own, other, log_weights, relaid)


def exchange(values, axes):
    return lax.all_to_all(values, axes, 0, 0, tiled=True)


def reversed_exchange(values, axes):
    order = list(range(values.shape[0]))[::-1]
    return lax.all_to_all(values, axes, 0, 0, tiled=True, axis_index_groups=[order])


def per_device(ensemble, log_weights):
    swap = [(0, 1), (1, 0)]
    rows, cells = ensemble.shape
    count = M // rows
    shape = (count, rows, cells // count)
    blocks = split_cells(ensemble, shape)
    relaid = reversed_exchange(blocks, MEM).reshape(M, cells // count)
    keep, send = partial_distances(relaid)
    recv = lax.ppermute(send, "core", swap)
    slabs = small_call(pack_kernel, (BLOCK_SIZE, SLAB, T), jnp.float32, "pack")(keep, recv)
    parts = exchange(slabs.astype(jnp.float16), BLOCK).astype(jnp.float32)
    strips = small_call(strip_kernel, (BLOCKS, SLAB, T), jnp.float32, "strip")(parts)
    parts = reversed_exchange(strips.astype(jnp.float16), "zo").astype(jnp.float32)
    entries = small_call(entries_kernel, (BLOCK_SIZE, SLAB, T), jnp.bfloat16, "entries")(parts)
    own = exchange(entries, BLOCK)
    other = lax.ppermute(own, "core", swap)
    mixed = analysis_members(own, other, log_weights.reshape(1, M), relaid)
    blocks = reversed_exchange(mixed.reshape(shape), MEM)
    return join_cells(blocks, ensemble.shape)


def solution(mesh):
    fine = Mesh(mesh.devices.reshape(8, 2, 2, 4, 4), ("zo", "zi", "core", "y", "x"))
    return jax.shard_map(
        per_device,
        mesh=fine,
        in_specs=(P(MEM, PLANE), P()),
        out_specs=P(MEM, PLANE),
        check_vma=False,
    )
```

```python
import jax
import jax.numpy as jnp
from jax import lax
from jax.experimental import pallas as pl
from jax.experimental.pallas import tpu as pltpu
from jax.sharding import Mesh
from jax.sharding import PartitionSpec as P

M = 1024
OWN = 32
ITERS = 10
T = 128
NB = M // T
TILES = [(i, j) for i in range(NB) for j in range(i, NB)]
HALF = len(TILES) // 2
ROWS = HALF * T
HEAD = 8
BLOCK_SIZE = 32
BLOCKS = 8
STRIP = ROWS // BLOCK_SIZE
SLAB = STRIP + HEAD
SPLIT = 512
GROUP = 16
MEM = ("zo", "zi", "core")
PLANE = ("y", "x")
BLOCK = ("zi", "y", "x")


def eye_mask():
    return lax.broadcasted_iota(jnp.int32, (T, T), 0) == lax.broadcasted_iota(jnp.int32, (T, T), 1)


def split_kernel(ensemble_ref, out_ref):
    count, _, cells = out_ref.shape
    for d in range(count):
        out_ref[d] = ensemble_ref[:, d * cells:(d + 1) * cells]


def join_kernel(blocks_ref, out_ref, sems):
    count, _, cells = blocks_ref.shape
    copies = [
        pltpu.make_async_copy(blocks_ref.at[d], out_ref.at[:, d * cells:(d + 1) * cells], sems.at[d])
        for d in range(count)
    ]
    for copy in copies:
        copy.start()
    for copy in copies:
        copy.wait()


def split_cells(ensemble, shape):
    return pl.pallas_call(
        split_kernel,
        out_shape=jax.ShapeDtypeStruct(shape, ensemble.dtype),
        in_specs=[pl.BlockSpec(memory_space=pltpu.VMEM)],
        out_specs=pl.BlockSpec(memory_space=pltpu.VMEM),
        compiler_params=pltpu.CompilerParams(vmem_limit_bytes=8 << 20),
        name="split",
    )(ensemble)


def join_cells(blocks, shape):
    return pl.pallas_call(
        join_kernel,
        out_shape=jax.ShapeDtypeStruct(shape, blocks.dtype),
        in_specs=[pl.BlockSpec(memory_space=pltpu.VMEM)],
        out_specs=pl.BlockSpec(memory_space=pltpu.HBM),
        scratch_shapes=[pltpu.SemaphoreType.DMA((blocks.shape[0],))],
        compiler_params=pltpu.CompilerParams(vmem_limit_bytes=8 << 20),
        name="join",
    )(blocks)


def distance_kernel(relaid_ref, keep_ref, send_ref, packed):
    core = lax.axis_index("core")
    eye = eye_mask()
    norm_row = {}
    diagonal = jnp.zeros((8, T), jnp.float32)
    upper = jnp.zeros((8, T), jnp.float32)
    largest = jnp.zeros((8, T), jnp.float32)
    for start in reversed(range(0, NB, 2)):
        strip = lax.dot_general(
            relaid_ref[start * T:(start + 2) * T, :], relaid_ref[start * T:, :],
            (((1,), (1,)), ((), ())), preferred_element_type=jnp.float32,
        )
        for i in (start + 1, start):
            rows = slice((i - start) * T, (i - start + 1) * T)
            own = jnp.where(eye, strip[rows, rows], 0.0)
            norm_row[i] = jnp.sum(own, axis=0, keepdims=True)
            norm_col = jnp.sum(own, axis=1, keepdims=True)
            for j in range(i, NB):
                half, slot = divmod(TILES.index((i, j)), HALF)
                gram = strip[rows, (j - start) * T:(j - start + 1) * T]
                value = norm_col + norm_row[j] - 2.0 * gram
                packed[half, slot * T:(slot + 1) * T, :] = value
                folded = value.reshape(T // 8, 8, T)
                largest = jnp.maximum(largest, jnp.max(folded, axis=0))
                if i == j:
                    diagonal += jnp.sum(folded, axis=0)
                else:
                    upper += jnp.sum(folded, axis=0)
    total = jnp.broadcast_to(jnp.sum(diagonal + 2.0 * upper, keepdims=True), (1, T))
    bound = jnp.broadcast_to(jnp.max(largest, keepdims=True), (1, T))
    power, scale = scaling(bound)
    row = lax.broadcasted_iota(jnp.int32, (HEAD, T), 0)
    keep_ref[:ROWS, :] = packed[core]
    keep_ref[ROWS:, :] = jnp.where(row == 0, total, jnp.where(row == 1, bound, 0.0))
    send_ref[:ROWS, :] = packed[1 - core] * scale
    send_ref[ROWS:, :] = tail_rows(power, scale, total)


def partial_distances(relaid):
    shape = jax.ShapeDtypeStruct((ROWS + HEAD, T), jnp.float32)
    vmem = pl.BlockSpec(memory_space=pltpu.VMEM)
    return pl.pallas_call(
        distance_kernel,
        out_shape=(shape, shape),
        in_specs=[vmem],
        out_specs=(vmem, vmem),
        scratch_shapes=[pltpu.VMEM((2, ROWS, T), jnp.float32)],
        compiler_params=pltpu.CompilerParams(vmem_limit_bytes=32 << 20),
        name="distances",
    )(relaid)


def scaling(bound):
    power = jnp.floor(15.0 - jnp.log2(jnp.maximum(bound, 1e-30)))
    return power, jnp.exp2(power)


def tail_rows(power, scale, total):
    share = total * scale * 2.0**-20
    high = share.astype(jnp.bfloat16).astype(jnp.float32)
    middle = (share - high).astype(jnp.bfloat16).astype(jnp.float32)
    low = share - high - middle
    row = lax.broadcasted_iota(jnp.int32, (HEAD, T), 0)
    tail = jnp.zeros((HEAD, T), jnp.float32)
    for index, value in enumerate((power, high, middle, low)):
        tail = jnp.where(row == index, value, tail)
    return tail


def tail_total(tail, inverse):
    return (tail[1:2, :] + tail[2:3, :] + tail[3:4, :]) * inverse * 2.0**20


def summed(parts_ref):
    acc = jnp.zeros((STRIP, T), jnp.float32)
    total = jnp.zeros((1, T), jnp.float32)
    for p in range(parts_ref.shape[0]):
        tail = parts_ref[p, STRIP:, :]
        inverse = jnp.exp2(-tail[0:1, :])
        acc += parts_ref[p, :STRIP, :] * inverse
        total += tail_total(tail, inverse)
    return acc, total


def pack_kernel(keep_ref, recv_ref, out_ref):
    other = recv_ref[ROWS:, :]
    inverse = jnp.exp2(-other[0:1, :])
    total = keep_ref[ROWS:ROWS + 1, :] + tail_total(other, inverse)
    power, scale = scaling(keep_ref[ROWS + 1:ROWS + 2, :] + jnp.exp2(15.0 - other[0:1, :]))
    tail = tail_rows(power, scale, total)
    for p in range(BLOCK_SIZE):
        rows = slice(p * STRIP, (p + 1) * STRIP)
        out_ref[p, :STRIP, :] = (keep_ref[rows, :] + recv_ref[rows, :] * inverse) * scale
        out_ref[p, STRIP:, :] = tail


def strip_kernel(parts_ref, out_ref):
    acc, total = summed(parts_ref)
    power, scale = scaling(jnp.maximum(jnp.max(acc, keepdims=True), total * 2.0**-20))
    tail = tail_rows(power, scale, total)
    acc = acc * scale
    for g in range(BLOCKS):
        out_ref[g, :STRIP, :] = acc
        out_ref[g, STRIP:, :] = tail


def entries_kernel(parts_ref, out_ref):
    acc, total = summed(parts_ref)
    mean = total / (M * (M - 1))
    entries = jnp.exp(acc * (-1.0 / (0.08 * mean)))
    entries = jnp.concatenate([entries, jnp.zeros((HEAD, T), jnp.float32)], axis=0)
    entries = entries.astype(jnp.bfloat16)
    for p in range(BLOCK_SIZE):
        out_ref[p, :, :] = entries


def small_call(body, shape, dtype, name):
    return pl.pallas_call(
        body,
        out_shape=jax.ShapeDtypeStruct(shape, dtype),
        compiler_params=pltpu.CompilerParams(vmem_limit_bytes=16 << 20),
        name=name,
    )


def analysis_kernel(own_ref, other_ref, logw_ref, relaid_ref, out_ref,
                    packed, kern_a, kern_at, kern_b, weight, scale, coup):
    core = lax.axis_index("core")
    for p in range(BLOCK_SIZE):
        rows = slice(p * STRIP, (p + 1) * STRIP)
        packed[core, rows, :] = own_ref[p].astype(jnp.float32)[:STRIP, :]
        packed[1 - core, rows, :] = other_ref[p].astype(jnp.float32)[:STRIP, :]

    def place(i, j, value):
        cols = slice(j * T, (j + 1) * T)
        if i * T < SPLIT:
            kern_a[i * T:(i + 1) * T, cols] = value.astype(jnp.bfloat16)
        else:
            kern_b[i * T - SPLIT:(i + 1) * T - SPLIT, cols] = value
        if j * T < SPLIT:
            kern_at[i * T:(i + 1) * T, cols] = value.astype(jnp.bfloat16)

    for tile, (i, j) in enumerate(TILES):
        half, slot = divmod(tile, HALF)
        value = packed[half, slot * T:(slot + 1) * T, :]
        place(i, j, value)
        if i != j:
            place(j, i, value.T)

    eye = eye_mask()

    def to_column(row):
        return jnp.broadcast_to(jnp.sum(jnp.where(eye, row, 0.0), axis=1, keepdims=True), (T, T))

    logw = logw_ref[...]
    expw = jnp.exp(logw - jnp.max(logw, axis=1, keepdims=True))
    weights = expw / jnp.sum(expw, axis=1, keepdims=True)
    weights = jnp.concatenate(
        [weights[:, k * OWN:(k + 1) * OWN] for k in reversed(range(M // OWN))], axis=1
    )
    for i in range(SPLIT // T, NB):
        weight[i * T - SPLIT:(i + 1) * T - SPLIT, :] = to_column(weights[:, i * T:(i + 1) * T])

    def product(vector, matrix):
        first = vector.astype(jnp.bfloat16).astype(jnp.float32)
        second = (vector - first).astype(jnp.bfloat16).astype(jnp.float32)
        third = vector - first - second
        row = lax.broadcasted_iota(jnp.int32, (16, vector.shape[1]), 0)
        parts = jnp.where(row == 0, first, jnp.where(row == 1, second, jnp.where(row == 2, third, 0.0)))
        sums = jnp.dot(parts.astype(jnp.bfloat16), matrix, preferred_element_type=jnp.float32)
        return sums[0:1, :] + sums[1:2, :] + sums[2:3, :]

    def sweep(step, scales):
        scale_col = scales[1]
        scale_a = weights[:, :SPLIT] / product(scale_col, kern_at[...])
        from_a = product(scale_a, kern_a[...])
        wide = [jnp.broadcast_to(scale_col[:, l * T:(l + 1) * T], (8, T)) for l in range(NB)]
        sums = [jnp.zeros((8, T), jnp.float32) for _ in range(NB)]
        for base in range(0, M - SPLIT, 8 * GROUP):
            row_scale = []
            for g in range(GROUP):
                rows = slice(base + 8 * g, base + 8 * g + 8)
                acc = kern_b[rows, 0:T] * wide[0]
                for l in range(1, NB):
                    acc += kern_b[rows, l * T:(l + 1) * T] * wide[l]
                r = weight[rows, :] / jnp.sum(acc, axis=1, keepdims=True)
                scale[rows, :] = r
                row_scale.append(r)
            for g in range(GROUP):
                rows = slice(base + 8 * g, base + 8 * g + 8)
                for l in range(NB):
                    sums[l] += kern_b[rows, l * T:(l + 1) * T] * row_scale[g]
        from_b = jnp.concatenate([jnp.sum(s, axis=0, keepdims=True) for s in sums], axis=1)
        return scale_a, (1.0 / M) / (from_a + from_b)

    start = (weights[:, :SPLIT], jnp.ones((1, M), jnp.float32))
    scale_a, scale_col = lax.fori_loop(0, ITERS, sweep, start)

    scale_row = [M * scale_a[:, i * T:(i + 1) * T] for i in range(SPLIT // T)]
    for i in range(SPLIT // T, NB):
        block = scale[i * T - SPLIT:(i + 1) * T - SPLIT, :]
        scale_row.append(M * jnp.sum(jnp.where(eye, block, 0.0), axis=0, keepdims=True))
    for j in range(NB):
        rows = slice(j * T, (j + 1) * T)
        column = to_column(scale_col[:, rows])
        for i in range(NB):
            cols = slice(i * T, (i + 1) * T)
            if j * T < SPLIT:
                value = kern_a[rows, cols].astype(jnp.float32)
            else:
                value = kern_b[j * T - SPLIT:(j + 1) * T - SPLIT, cols]
            coup[rows, cols] = (scale_row[i] * value * column).astype(jnp.bfloat16)
    for j in range(0, NB, 2):
        mixed = jnp.dot(
            coup[j * T:(j + 2) * T, :], relaid_ref[...], preferred_element_type=jnp.float32
        )
        out_ref[j * T:(j + 2) * T, :] = mixed.astype(jnp.bfloat16)


def analysis_members(own, other, log_weights, relaid):
    vmem = pl.BlockSpec(memory_space=pltpu.VMEM)
    return pl.pallas_call(
        analysis_kernel,
        out_shape=jax.ShapeDtypeStruct(relaid.shape, jnp.bfloat16),
        in_specs=[vmem, vmem, vmem, vmem],
        out_specs=vmem,
        scratch_shapes=[
            pltpu.VMEM((2, ROWS, T), jnp.float32),
            pltpu.VMEM((SPLIT, M), jnp.bfloat16),
            pltpu.VMEM((M, SPLIT), jnp.bfloat16),
            pltpu.VMEM((M - SPLIT, M), jnp.float32),
            pltpu.VMEM((M - SPLIT, T), jnp.float32),
            pltpu.VMEM((M - SPLIT, T), jnp.float32),
            pltpu.VMEM((M, M), jnp.bfloat16),
        ],
        compiler_params=pltpu.CompilerParams(vmem_limit_bytes=40 << 20),
        name="analysis",
    )(own, other, log_weights, relaid)


def exchange(values, axes):
    return lax.all_to_all(values, axes, 0, 0, tiled=True)


def reversed_exchange(values, axes):
    order = list(range(values.shape[0]))[::-1]
    return lax.all_to_all(values, axes, 0, 0, tiled=True, axis_index_groups=[order])


def per_device(ensemble, log_weights):
    swap = [(0, 1), (1, 0)]
    rows, cells = ensemble.shape
    count = M // rows
    shape = (count, rows, cells // count)
    blocks = split_cells(ensemble, shape)
    relaid = reversed_exchange(blocks, MEM).reshape(M, cells // count)
    keep, send = partial_distances(relaid)
    recv = lax.ppermute(send.astype(jnp.float16), "core", swap).astype(jnp.float32)
    slabs = small_call(pack_kernel, (BLOCK_SIZE, SLAB, T), jnp.float32, "pack")(keep, recv)
    parts = exchange(slabs.astype(jnp.float16), BLOCK).astype(jnp.float32)
    strips = small_call(strip_kernel, (BLOCKS, SLAB, T), jnp.float32, "strip")(parts)
    parts = reversed_exchange(strips.astype(jnp.float16), "zo").astype(jnp.float32)
    entries = small_call(entries_kernel, (BLOCK_SIZE, SLAB, T), jnp.bfloat16, "entries")(parts)
    own = exchange(entries, BLOCK)
    other = lax.ppermute(own, "core", swap)
    mixed = analysis_members(own, other, log_weights.reshape(1, M), relaid)
    blocks = reversed_exchange(mixed.reshape(shape), MEM)
    return join_cells(blocks, ensemble.shape)


def solution(mesh):
    fine = Mesh(mesh.devices.reshape(8, 2, 2, 4, 4), ("zo", "zi", "core", "y", "x"))
    return jax.shard_map(
        per_device,
        mesh=fine,
        in_specs=(P(MEM, PLANE), P()),
        out_specs=P(MEM, PLANE),
        check_vma=False,
    )
```

```python
import jax
import jax.numpy as jnp
from jax import lax
from jax.experimental import pallas as pl
from jax.experimental.pallas import tpu as pltpu
from jax.sharding import Mesh
from jax.sharding import PartitionSpec as P

M = 1024
OWN = 32
ORDER = [2 * z + core for core in range(2) for z in reversed(range(16))]
ITERS = 10
T = 128
NB = M // T
TILES = [(i, j) for i in range(NB) for j in range(i, NB)]
HALF = len(TILES) // 2
ROWS = HALF * T
HEAD = 8
BLOCK_SIZE = 32
BLOCKS = 8
STRIP = ROWS // BLOCK_SIZE
SLAB = STRIP + HEAD
SPLIT = 512
GROUP = 16
MEM = ("zo", "zi", "core")
PLANE = ("y", "x")
BLOCK = ("zi", "y", "x")


def eye_mask():
    return lax.broadcasted_iota(jnp.int32, (T, T), 0) == lax.broadcasted_iota(jnp.int32, (T, T), 1)


def split_kernel(ensemble_ref, out_ref):
    count, _, cells = out_ref.shape
    for d in range(count):
        out_ref[d] = ensemble_ref[:, d * cells:(d + 1) * cells]


def join_kernel(blocks_ref, out_ref, sems):
    count, _, cells = blocks_ref.shape
    copies = [
        pltpu.make_async_copy(blocks_ref.at[d], out_ref.at[:, d * cells:(d + 1) * cells], sems.at[d])
        for d in range(count)
    ]
    for copy in copies:
        copy.start()
    for copy in copies:
        copy.wait()


def split_cells(ensemble, shape):
    return pl.pallas_call(
        split_kernel,
        out_shape=jax.ShapeDtypeStruct(shape, ensemble.dtype),
        in_specs=[pl.BlockSpec(memory_space=pltpu.VMEM)],
        out_specs=pl.BlockSpec(memory_space=pltpu.VMEM),
        compiler_params=pltpu.CompilerParams(vmem_limit_bytes=8 << 20),
        name="split",
    )(ensemble)


def join_cells(blocks, shape):
    return pl.pallas_call(
        join_kernel,
        out_shape=jax.ShapeDtypeStruct(shape, blocks.dtype),
        in_specs=[pl.BlockSpec(memory_space=pltpu.VMEM)],
        out_specs=pl.BlockSpec(memory_space=pltpu.HBM),
        scratch_shapes=[pltpu.SemaphoreType.DMA((blocks.shape[0],))],
        compiler_params=pltpu.CompilerParams(vmem_limit_bytes=8 << 20),
        name="join",
    )(blocks)


def distance_kernel(relaid_ref, keep_ref, send_ref, packed):
    core = lax.axis_index("core")
    eye = eye_mask()
    norm_row = {}
    diagonal = jnp.zeros((8, T), jnp.float32)
    upper = jnp.zeros((8, T), jnp.float32)
    largest = jnp.zeros((8, T), jnp.float32)
    for start in reversed(range(0, NB, 2)):
        strip = lax.dot_general(
            relaid_ref[start * T:(start + 2) * T, :], relaid_ref[start * T:, :],
            (((1,), (1,)), ((), ())), preferred_element_type=jnp.float32,
        )
        for i in (start + 1, start):
            rows = slice((i - start) * T, (i - start + 1) * T)
            own = jnp.where(eye, strip[rows, rows], 0.0)
            norm_row[i] = jnp.sum(own, axis=0, keepdims=True)
            norm_col = jnp.sum(own, axis=1, keepdims=True)
            for j in range(i, NB):
                half, slot = divmod(TILES.index((i, j)), HALF)
                gram = strip[rows, (j - start) * T:(j - start + 1) * T]
                value = norm_col + norm_row[j] - 2.0 * gram
                packed[half, slot * T:(slot + 1) * T, :] = value
                folded = value.reshape(T // 8, 8, T)
                largest = jnp.maximum(largest, jnp.max(folded, axis=0))
                if i == j:
                    diagonal += jnp.sum(folded, axis=0)
                else:
                    upper += jnp.sum(folded, axis=0)
    total = jnp.broadcast_to(jnp.sum(diagonal + 2.0 * upper, keepdims=True), (1, T))
    bound = jnp.broadcast_to(jnp.max(largest, keepdims=True), (1, T))
    power, scale = scaling(bound)
    row = lax.broadcasted_iota(jnp.int32, (HEAD, T), 0)
    keep_ref[:ROWS, :] = packed[core]
    keep_ref[ROWS:, :] = jnp.where(row == 0, total, jnp.where(row == 1, bound, 0.0))
    send_ref[:ROWS, :] = packed[1 - core] * scale
    send_ref[ROWS:, :] = tail_rows(power, scale, total)


def partial_distances(relaid):
    shape = jax.ShapeDtypeStruct((ROWS + HEAD, T), jnp.float32)
    vmem = pl.BlockSpec(memory_space=pltpu.VMEM)
    return pl.pallas_call(
        distance_kernel,
        out_shape=(shape, shape),
        in_specs=[vmem],
        out_specs=(vmem, vmem),
        scratch_shapes=[pltpu.VMEM((2, ROWS, T), jnp.float32)],
        compiler_params=pltpu.CompilerParams(vmem_limit_bytes=32 << 20),
        name="distances",
    )(relaid)


def scaling(bound):
    power = jnp.floor(15.0 - jnp.log2(jnp.maximum(bound, 1e-30)))
    return power, jnp.exp2(power)


def tail_rows(power, scale, total):
    share = total * scale * 2.0**-20
    high = share.astype(jnp.bfloat16).astype(jnp.float32)
    middle = (share - high).astype(jnp.bfloat16).astype(jnp.float32)
    low = share - high - middle
    row = lax.broadcasted_iota(jnp.int32, (HEAD, T), 0)
    tail = jnp.zeros((HEAD, T), jnp.float32)
    for index, value in enumerate((power, high, middle, low)):
        tail = jnp.where(row == index, value, tail)
    return tail


def tail_total(tail, inverse):
    return (tail[1:2, :] + tail[2:3, :] + tail[3:4, :]) * inverse * 2.0**20


def summed(parts_ref):
    acc = jnp.zeros((STRIP, T), jnp.float32)
    total = jnp.zeros((1, T), jnp.float32)
    for p in range(parts_ref.shape[0]):
        tail = parts_ref[p, STRIP:, :]
        inverse = jnp.exp2(-tail[0:1, :])
        acc += parts_ref[p, :STRIP, :] * inverse
        total += tail_total(tail, inverse)
    return acc, total


def pack_kernel(keep_ref, recv_ref, out_ref):
    other = recv_ref[ROWS:, :]
    inverse = jnp.exp2(-other[0:1, :])
    total = keep_ref[ROWS:ROWS + 1, :] + tail_total(other, inverse)
    power, scale = scaling(keep_ref[ROWS + 1:ROWS + 2, :] + jnp.exp2(15.0 - other[0:1, :]))
    tail = tail_rows(power, scale, total)
    for p in range(BLOCK_SIZE):
        rows = slice(p * STRIP, (p + 1) * STRIP)
        out_ref[p, :STRIP, :] = (keep_ref[rows, :] + recv_ref[rows, :] * inverse) * scale
        out_ref[p, STRIP:, :] = tail


def strip_kernel(parts_ref, out_ref):
    acc, total = summed(parts_ref)
    power, scale = scaling(jnp.maximum(jnp.max(acc, keepdims=True), total * 2.0**-20))
    tail = tail_rows(power, scale, total)
    acc = acc * scale
    for g in range(BLOCKS):
        out_ref[g, :STRIP, :] = acc
        out_ref[g, STRIP:, :] = tail


def entries_kernel(parts_ref, out_ref):
    acc, total = summed(parts_ref)
    mean = total / (M * (M - 1))
    entries = jnp.exp(acc * (-1.0 / (0.08 * mean)))
    entries = jnp.concatenate([entries, jnp.zeros((HEAD, T), jnp.float32)], axis=0)
    entries = entries.astype(jnp.bfloat16)
    for p in range(BLOCK_SIZE):
        out_ref[p, :, :] = entries


def small_call(body, shape, dtype, name):
    return pl.pallas_call(
        body,
        out_shape=jax.ShapeDtypeStruct(shape, dtype),
        compiler_params=pltpu.CompilerParams(vmem_limit_bytes=16 << 20),
        name=name,
    )


def analysis_kernel(own_ref, other_ref, logw_ref, relaid_ref, out_ref,
                    packed, kern_a, kern_at, kern_b, weight, scale, coup):
    core = lax.axis_index("core")
    for p in range(BLOCK_SIZE):
        rows = slice(p * STRIP, (p + 1) * STRIP)
        packed[core, rows, :] = own_ref[p].astype(jnp.float32)[:STRIP, :]
        packed[1 - core, rows, :] = other_ref[p].astype(jnp.float32)[:STRIP, :]

    def place(i, j, value):
        cols = slice(j * T, (j + 1) * T)
        if i * T < SPLIT:
            kern_a[i * T:(i + 1) * T, cols] = value.astype(jnp.bfloat16)
        else:
            kern_b[i * T - SPLIT:(i + 1) * T - SPLIT, cols] = value
        if j * T < SPLIT:
            kern_at[i * T:(i + 1) * T, cols] = value.astype(jnp.bfloat16)

    for tile, (i, j) in enumerate(TILES):
        half, slot = divmod(tile, HALF)
        value = packed[half, slot * T:(slot + 1) * T, :]
        place(i, j, value)
        if i != j:
            place(j, i, value.T)

    eye = eye_mask()

    def to_column(row):
        return jnp.broadcast_to(jnp.sum(jnp.where(eye, row, 0.0), axis=1, keepdims=True), (T, T))

    logw = logw_ref[...]
    expw = jnp.exp(logw - jnp.max(logw, axis=1, keepdims=True))
    weights = expw / jnp.sum(expw, axis=1, keepdims=True)
    weights = jnp.concatenate([weights[:, k * OWN:(k + 1) * OWN] for k in ORDER], axis=1)
    for i in range(SPLIT // T, NB):
        weight[i * T - SPLIT:(i + 1) * T - SPLIT, :] = to_column(weights[:, i * T:(i + 1) * T])

    def product(vector, matrix):
        first = vector.astype(jnp.bfloat16).astype(jnp.float32)
        second = (vector - first).astype(jnp.bfloat16).astype(jnp.float32)
        third = vector - first - second
        row = lax.broadcasted_iota(jnp.int32, (16, vector.shape[1]), 0)
        parts = jnp.where(row == 0, first, jnp.where(row == 1, second, jnp.where(row == 2, third, 0.0)))
        sums = jnp.dot(parts.astype(jnp.bfloat16), matrix, preferred_element_type=jnp.float32)
        return sums[0:1, :] + sums[1:2, :] + sums[2:3, :]

    def sweep(step, scales):
        scale_col = scales[1]
        scale_a = weights[:, :SPLIT] / product(scale_col, kern_at[...])
        from_a = product(scale_a, kern_a[...])
        wide = [jnp.broadcast_to(scale_col[:, l * T:(l + 1) * T], (8, T)) for l in range(NB)]
        sums = [jnp.zeros((8, T), jnp.float32) for _ in range(NB)]
        for base in range(0, M - SPLIT, 8 * GROUP):
            row_scale = []
            for g in range(GROUP):
                rows = slice(base + 8 * g, base + 8 * g + 8)
                acc = kern_b[rows, 0:T] * wide[0]
                for l in range(1, NB):
                    acc += kern_b[rows, l * T:(l + 1) * T] * wide[l]
                r = weight[rows, :] / jnp.sum(acc, axis=1, keepdims=True)
                scale[rows, :] = r
                row_scale.append(r)
            for g in range(GROUP):
                rows = slice(base + 8 * g, base + 8 * g + 8)
                for l in range(NB):
                    sums[l] += kern_b[rows, l * T:(l + 1) * T] * row_scale[g]
        from_b = jnp.concatenate([jnp.sum(s, axis=0, keepdims=True) for s in sums], axis=1)
        return scale_a, (1.0 / M) / (from_a + from_b)

    start = (weights[:, :SPLIT], jnp.ones((1, M), jnp.float32))
    scale_a, scale_col = lax.fori_loop(0, ITERS, sweep, start)

    scale_row = [M * scale_a[:, i * T:(i + 1) * T] for i in range(SPLIT // T)]
    for i in range(SPLIT // T, NB):
        block = scale[i * T - SPLIT:(i + 1) * T - SPLIT, :]
        scale_row.append(M * jnp.sum(jnp.where(eye, block, 0.0), axis=0, keepdims=True))
    for j in range(NB):
        rows = slice(j * T, (j + 1) * T)
        column = to_column(scale_col[:, rows])
        for i in range(NB):
            cols = slice(i * T, (i + 1) * T)
            if j * T < SPLIT:
                value = kern_a[rows, cols].astype(jnp.float32)
            else:
                value = kern_b[j * T - SPLIT:(j + 1) * T - SPLIT, cols]
            coup[rows, cols] = (scale_row[i] * value * column).astype(jnp.bfloat16)
    for j in range(0, NB, 2):
        mixed = jnp.dot(
            coup[j * T:(j + 2) * T, :], relaid_ref[...], preferred_element_type=jnp.float32
        )
        out_ref[j * T:(j + 2) * T, :] = mixed.astype(jnp.bfloat16)


def analysis_members(own, other, log_weights, relaid):
    vmem = pl.BlockSpec(memory_space=pltpu.VMEM)
    return pl.pallas_call(
        analysis_kernel,
        out_shape=jax.ShapeDtypeStruct(relaid.shape, jnp.bfloat16),
        in_specs=[vmem, vmem, vmem, vmem],
        out_specs=vmem,
        scratch_shapes=[
            pltpu.VMEM((2, ROWS, T), jnp.float32),
            pltpu.VMEM((SPLIT, M), jnp.bfloat16),
            pltpu.VMEM((M, SPLIT), jnp.bfloat16),
            pltpu.VMEM((M - SPLIT, M), jnp.float32),
            pltpu.VMEM((M - SPLIT, T), jnp.float32),
            pltpu.VMEM((M - SPLIT, T), jnp.float32),
            pltpu.VMEM((M, M), jnp.bfloat16),
        ],
        compiler_params=pltpu.CompilerParams(vmem_limit_bytes=40 << 20),
        name="analysis",
    )(own, other, log_weights, relaid)


def exchange(values, axes):
    return lax.all_to_all(values, axes, 0, 0, tiled=True)


def ordered_exchange(values, axes, order):
    return lax.all_to_all(values, axes, 0, 0, tiled=True, axis_index_groups=[order])


def per_device(ensemble, log_weights):
    swap = [(0, 1), (1, 0)]
    rows, cells = ensemble.shape
    count = M // rows
    shape = (count, rows, cells // count)
    blocks = split_cells(ensemble, shape)
    relaid = ordered_exchange(blocks, MEM, ORDER).reshape(M, cells // count)
    keep, send = partial_distances(relaid)
    recv = lax.ppermute(send.astype(jnp.float16), "core", swap).astype(jnp.float32)
    slabs = small_call(pack_kernel, (BLOCK_SIZE, SLAB, T), jnp.float32, "pack")(keep, recv)
    parts = exchange(slabs.astype(jnp.float16), BLOCK).astype(jnp.float32)
    strips = small_call(strip_kernel, (BLOCKS, SLAB, T), jnp.float32, "strip")(parts)
    parts = ordered_exchange(strips.astype(jnp.float16), "zo", list(range(BLOCKS))[::-1]).astype(jnp.float32)
    entries = small_call(entries_kernel, (BLOCK_SIZE, SLAB, T), jnp.bfloat16, "entries")(parts)
    own = exchange(entries, BLOCK)
    other = lax.ppermute(own, "core", swap)
    mixed = analysis_members(own, other, log_weights.reshape(1, M), relaid)
    blocks = ordered_exchange(mixed.reshape(shape), MEM, ORDER)
    return join_cells(blocks, ensemble.shape)


def solution(mesh):
    fine = Mesh(mesh.devices.reshape(8, 2, 2, 4, 4), ("zo", "zi", "core", "y", "x"))
    return jax.shard_map(
        per_device,
        mesh=fine,
        in_specs=(P(MEM, PLANE), P()),
        out_specs=P(MEM, PLANE),
        check_vma=False,
    )
```

```python
import jax
import jax.numpy as jnp
from jax import lax
from jax.experimental import pallas as pl
from jax.experimental.pallas import tpu as pltpu
from jax.sharding import Mesh
from jax.sharding import PartitionSpec as P

M = 1024
OWN = 32
ORDER = [2 * z + core for core in (1, 0) for z in reversed(range(16))]
ITERS = 10
T = 128
NB = M // T
TILES = [(i, j) for i in range(NB) for j in range(i, NB)]
HALF = len(TILES) // 2
ROWS = HALF * T
HEAD = 8
BLOCK_SIZE = 32
BLOCKS = 8
STRIP = ROWS // BLOCK_SIZE
SLAB = STRIP + HEAD
SPLIT = 512
GROUP = 16
MEM = ("zo", "zi", "core")
PLANE = ("y", "x")
BLOCK = ("zi", "y", "x")


def eye_mask():
    return lax.broadcasted_iota(jnp.int32, (T, T), 0) == lax.broadcasted_iota(jnp.int32, (T, T), 1)


def split_kernel(ensemble_ref, out_ref):
    count, _, cells = out_ref.shape
    for d in range(count):
        out_ref[d] = ensemble_ref[:, d * cells:(d + 1) * cells]


def join_kernel(blocks_ref, out_ref, sems):
    count, _, cells = blocks_ref.shape
    copies = [
        pltpu.make_async_copy(blocks_ref.at[d], out_ref.at[:, d * cells:(d + 1) * cells], sems.at[d])
        for d in range(count)
    ]
    for copy in copies:
        copy.start()
    for copy in copies:
        copy.wait()


def split_cells(ensemble, shape):
    return pl.pallas_call(
        split_kernel,
        out_shape=jax.ShapeDtypeStruct(shape, ensemble.dtype),
        in_specs=[pl.BlockSpec(memory_space=pltpu.VMEM)],
        out_specs=pl.BlockSpec(memory_space=pltpu.VMEM),
        compiler_params=pltpu.CompilerParams(vmem_limit_bytes=8 << 20),
        name="split",
    )(ensemble)


def join_cells(blocks, shape):
    return pl.pallas_call(
        join_kernel,
        out_shape=jax.ShapeDtypeStruct(shape, blocks.dtype),
        in_specs=[pl.BlockSpec(memory_space=pltpu.VMEM)],
        out_specs=pl.BlockSpec(memory_space=pltpu.HBM),
        scratch_shapes=[pltpu.SemaphoreType.DMA((blocks.shape[0],))],
        compiler_params=pltpu.CompilerParams(vmem_limit_bytes=8 << 20),
        name="join",
    )(blocks)


def distance_kernel(relaid_ref, keep_ref, send_ref, packed):
    core = lax.axis_index("core")
    eye = eye_mask()
    norm_row = {}
    diagonal = jnp.zeros((8, T), jnp.float32)
    upper = jnp.zeros((8, T), jnp.float32)
    largest = jnp.zeros((8, T), jnp.float32)
    for start in reversed(range(0, NB, 2)):
        strip = lax.dot_general(
            relaid_ref[start * T:(start + 2) * T, :], relaid_ref[start * T:, :],
            (((1,), (1,)), ((), ())), preferred_element_type=jnp.float32,
        )
        for i in (start + 1, start):
            rows = slice((i - start) * T, (i - start + 1) * T)
            own = jnp.where(eye, strip[rows, rows], 0.0)
            norm_row[i] = jnp.sum(own, axis=0, keepdims=True)
            norm_col = jnp.sum(own, axis=1, keepdims=True)
            for j in range(i, NB):
                half, slot = divmod(TILES.index((i, j)), HALF)
                gram = strip[rows, (j - start) * T:(j - start + 1) * T]
                value = norm_col + norm_row[j] - 2.0 * gram
                packed[half, slot * T:(slot + 1) * T, :] = value
                folded = value.reshape(T // 8, 8, T)
                largest = jnp.maximum(largest, jnp.max(folded, axis=0))
                if i == j:
                    diagonal += jnp.sum(folded, axis=0)
                else:
                    upper += jnp.sum(folded, axis=0)
    total = jnp.broadcast_to(jnp.sum(diagonal + 2.0 * upper, keepdims=True), (1, T))
    bound = jnp.broadcast_to(jnp.max(largest, keepdims=True), (1, T))
    power, scale = scaling(bound)
    row = lax.broadcasted_iota(jnp.int32, (HEAD, T), 0)
    keep_ref[:ROWS, :] = packed[core]
    keep_ref[ROWS:, :] = jnp.where(row == 0, total, jnp.where(row == 1, bound, 0.0))
    send_ref[:ROWS, :] = packed[1 - core] * scale
    send_ref[ROWS:, :] = tail_rows(power, scale, total)


def partial_distances(relaid):
    shape = jax.ShapeDtypeStruct((ROWS + HEAD, T), jnp.float32)
    vmem = pl.BlockSpec(memory_space=pltpu.VMEM)
    return pl.pallas_call(
        distance_kernel,
        out_shape=(shape, shape),
        in_specs=[vmem],
        out_specs=(vmem, vmem),
        scratch_shapes=[pltpu.VMEM((2, ROWS, T), jnp.float32)],
        compiler_params=pltpu.CompilerParams(vmem_limit_bytes=32 << 20),
        name="distances",
    )(relaid)


def scaling(bound):
    power = jnp.floor(15.0 - jnp.log2(jnp.maximum(bound, 1e-30)))
    return power, jnp.exp2(power)


def tail_rows(power, scale, total):
    share = total * scale * 2.0**-20
    high = share.astype(jnp.bfloat16).astype(jnp.float32)
    middle = (share - high).astype(jnp.bfloat16).astype(jnp.float32)
    low = share - high - middle
    row = lax.broadcasted_iota(jnp.int32, (HEAD, T), 0)
    tail = jnp.zeros((HEAD, T), jnp.float32)
    for index, value in enumerate((power, high, middle, low)):
        tail = jnp.where(row == index, value, tail)
    return tail


def tail_total(tail, inverse):
    return (tail[1:2, :] + tail[2:3, :] + tail[3:4, :]) * inverse * 2.0**20


def summed(parts_ref):
    acc = jnp.zeros((STRIP, T), jnp.float32)
    total = jnp.zeros((1, T), jnp.float32)
    for p in range(parts_ref.shape[0]):
        tail = parts_ref[p, STRIP:, :]
        inverse = jnp.exp2(-tail[0:1, :])
        acc += parts_ref[p, :STRIP, :] * inverse
        total += tail_total(tail, inverse)
    return acc, total


def pack_kernel(keep_ref, recv_ref, out_ref):
    other = recv_ref[ROWS:, :]
    inverse = jnp.exp2(-other[0:1, :])
    total = keep_ref[ROWS:ROWS + 1, :] + tail_total(other, inverse)
    power, scale = scaling(keep_ref[ROWS + 1:ROWS + 2, :] + jnp.exp2(15.0 - other[0:1, :]))
    tail = tail_rows(power, scale, total)
    for p in range(BLOCK_SIZE):
        rows = slice(p * STRIP, (p + 1) * STRIP)
        out_ref[p, :STRIP, :] = (keep_ref[rows, :] + recv_ref[rows, :] * inverse) * scale
        out_ref[p, STRIP:, :] = tail


def strip_kernel(parts_ref, out_ref):
    acc, total = summed(parts_ref)
    power, scale = scaling(jnp.maximum(jnp.max(acc, keepdims=True), total * 2.0**-20))
    tail = tail_rows(power, scale, total)
    acc = acc * scale
    for g in range(BLOCKS):
        out_ref[g, :STRIP, :] = acc
        out_ref[g, STRIP:, :] = tail


def entries_kernel(parts_ref, out_ref):
    acc, total = summed(parts_ref)
    mean = total / (M * (M - 1))
    entries = jnp.exp(acc * (-1.0 / (0.08 * mean)))
    entries = jnp.concatenate([entries, jnp.zeros((HEAD, T), jnp.float32)], axis=0)
    entries = entries.astype(jnp.bfloat16)
    for p in range(BLOCK_SIZE):
        out_ref[p, :, :] = entries


def small_call(body, shape, dtype, name):
    return pl.pallas_call(
        body,
        out_shape=jax.ShapeDtypeStruct(shape, dtype),
        compiler_params=pltpu.CompilerParams(vmem_limit_bytes=16 << 20),
        name=name,
    )


def analysis_kernel(own_ref, other_ref, logw_ref, relaid_ref, out_ref,
                    packed, kern_a, kern_at, kern_b, weight, scale, coup):
    core = lax.axis_index("core")
    for p in range(BLOCK_SIZE):
        rows = slice(p * STRIP, (p + 1) * STRIP)
        packed[core, rows, :] = own_ref[p].astype(jnp.float32)[:STRIP, :]
        packed[1 - core, rows, :] = other_ref[p].astype(jnp.float32)[:STRIP, :]

    def place(i, j, value):
        cols = slice(j * T, (j + 1) * T)
        if i * T < SPLIT:
            kern_a[i * T:(i + 1) * T, cols] = value.astype(jnp.bfloat16)
        else:
            kern_b[i * T - SPLIT:(i + 1) * T - SPLIT, cols] = value
        if j * T < SPLIT:
            kern_at[i * T:(i + 1) * T, cols] = value.astype(jnp.bfloat16)

    for tile, (i, j) in enumerate(TILES):
        half, slot = divmod(tile, HALF)
        value = packed[half, slot * T:(slot + 1) * T, :]
        place(i, j, value)
        if i != j:
            place(j, i, value.T)

    eye = eye_mask()

    def to_column(row):
        return jnp.broadcast_to(jnp.sum(jnp.where(eye, row, 0.0), axis=1, keepdims=True), (T, T))

    logw = logw_ref[...]
    expw = jnp.exp(logw - jnp.max(logw, axis=1, keepdims=True))
    weights = expw / jnp.sum(expw, axis=1, keepdims=True)
    weights = jnp.concatenate([weights[:, k * OWN:(k + 1) * OWN] for k in ORDER], axis=1)
    for i in range(SPLIT // T, NB):
        weight[i * T - SPLIT:(i + 1) * T - SPLIT, :] = to_column(weights[:, i * T:(i + 1) * T])

    def product(vector, matrix):
        first = vector.astype(jnp.bfloat16).astype(jnp.float32)
        second = (vector - first).astype(jnp.bfloat16).astype(jnp.float32)
        third = vector - first - second
        row = lax.broadcasted_iota(jnp.int32, (16, vector.shape[1]), 0)
        parts = jnp.where(row == 0, first, jnp.where(row == 1, second, jnp.where(row == 2, third, 0.0)))
        sums = jnp.dot(parts.astype(jnp.bfloat16), matrix, preferred_element_type=jnp.float32)
        return sums[0:1, :] + sums[1:2, :] + sums[2:3, :]

    def sweep(step, scales):
        scale_col = scales[1]
        scale_a = weights[:, :SPLIT] / product(scale_col, kern_at[...])
        from_a = product(scale_a, kern_a[...])
        wide = [jnp.broadcast_to(scale_col[:, l * T:(l + 1) * T], (8, T)) for l in range(NB)]
        sums = [jnp.zeros((8, T), jnp.float32) for _ in range(NB)]
        for base in range(0, M - SPLIT, 8 * GROUP):
            row_scale = []
            for g in range(GROUP):
                rows = slice(base + 8 * g, base + 8 * g + 8)
                acc = kern_b[rows, 0:T] * wide[0]
                for l in range(1, NB):
                    acc += kern_b[rows, l * T:(l + 1) * T] * wide[l]
                r = weight[rows, :] / jnp.sum(acc, axis=1, keepdims=True)
                scale[rows, :] = r
                row_scale.append(r)
            for g in range(GROUP):
                rows = slice(base + 8 * g, base + 8 * g + 8)
                for l in range(NB):
                    sums[l] += kern_b[rows, l * T:(l + 1) * T] * row_scale[g]
        from_b = jnp.concatenate([jnp.sum(s, axis=0, keepdims=True) for s in sums], axis=1)
        return scale_a, (1.0 / M) / (from_a + from_b)

    start = (weights[:, :SPLIT], jnp.ones((1, M), jnp.float32))
    scale_a, scale_col = lax.fori_loop(0, ITERS, sweep, start)

    scale_row = [M * scale_a[:, i * T:(i + 1) * T] for i in range(SPLIT // T)]
    for i in range(SPLIT // T, NB):
        block = scale[i * T - SPLIT:(i + 1) * T - SPLIT, :]
        scale_row.append(M * jnp.sum(jnp.where(eye, block, 0.0), axis=0, keepdims=True))
    for j in range(NB):
        rows = slice(j * T, (j + 1) * T)
        column = to_column(scale_col[:, rows])
        for i in range(NB):
            cols = slice(i * T, (i + 1) * T)
            if j * T < SPLIT:
                value = kern_a[rows, cols].astype(jnp.float32)
            else:
                value = kern_b[j * T - SPLIT:(j + 1) * T - SPLIT, cols]
            coup[rows, cols] = (scale_row[i] * value * column).astype(jnp.bfloat16)
    for j in range(0, NB, 2):
        mixed = jnp.dot(
            coup[j * T:(j + 2) * T, :], relaid_ref[...], preferred_element_type=jnp.float32
        )
        out_ref[j * T:(j + 2) * T, :] = mixed.astype(jnp.bfloat16)


def analysis_members(own, other, log_weights, relaid):
    vmem = pl.BlockSpec(memory_space=pltpu.VMEM)
    return pl.pallas_call(
        analysis_kernel,
        out_shape=jax.ShapeDtypeStruct(relaid.shape, jnp.bfloat16),
        in_specs=[vmem, vmem, vmem, vmem],
        out_specs=vmem,
        scratch_shapes=[
            pltpu.VMEM((2, ROWS, T), jnp.float32),
            pltpu.VMEM((SPLIT, M), jnp.bfloat16),
            pltpu.VMEM((M, SPLIT), jnp.bfloat16),
            pltpu.VMEM((M - SPLIT, M), jnp.float32),
            pltpu.VMEM((M - SPLIT, T), jnp.float32),
            pltpu.VMEM((M - SPLIT, T), jnp.float32),
            pltpu.VMEM((M, M), jnp.bfloat16),
        ],
        compiler_params=pltpu.CompilerParams(vmem_limit_bytes=40 << 20),
        name="analysis",
    )(own, other, log_weights, relaid)


def exchange(values, axes):
    return lax.all_to_all(values, axes, 0, 0, tiled=True)


def ordered_exchange(values, axes, order):
    return lax.all_to_all(values, axes, 0, 0, tiled=True, axis_index_groups=[order])


def per_device(ensemble, log_weights):
    swap = [(0, 1), (1, 0)]
    rows, cells = ensemble.shape
    count = M // rows
    shape = (count, rows, cells // count)
    blocks = split_cells(ensemble, shape)
    relaid = ordered_exchange(blocks, MEM, ORDER).reshape(M, cells // count)
    keep, send = partial_distances(relaid)
    recv = lax.ppermute(send.astype(jnp.float16), "core", swap).astype(jnp.float32)
    slabs = small_call(pack_kernel, (BLOCK_SIZE, SLAB, T), jnp.float32, "pack")(keep, recv)
    parts = exchange(slabs.astype(jnp.float16), BLOCK).astype(jnp.float32)
    strips = small_call(strip_kernel, (BLOCKS, SLAB, T), jnp.float32, "strip")(parts)
    parts = ordered_exchange(strips.astype(jnp.float16), "zo", list(range(BLOCKS))[::-1]).astype(jnp.float32)
    entries = small_call(entries_kernel, (BLOCK_SIZE, SLAB, T), jnp.bfloat16, "entries")(parts)
    own = exchange(entries, BLOCK)
    other = lax.ppermute(own, "core", swap)
    mixed = analysis_members(own, other, log_weights.reshape(1, M), relaid)
    blocks = ordered_exchange(mixed.reshape(shape), MEM, ORDER)
    return join_cells(blocks, ensemble.shape)


def solution(mesh):
    fine = Mesh(mesh.devices.reshape(8, 2, 2, 4, 4), ("zo", "zi", "core", "y", "x"))
    return jax.shard_map(
        per_device,
        mesh=fine,
        in_specs=(P(MEM, PLANE), P()),
        out_specs=P(MEM, PLANE),
        check_vma=False,
    )
```

```python
import jax
import jax.numpy as jnp
from jax import lax
from jax.experimental import pallas as pl
from jax.experimental.pallas import tpu as pltpu
from jax.sharding import Mesh
from jax.sharding import PartitionSpec as P

M = 1024
OWN = 32
ORDER = [2 * z + core for core in (1, 0) for z in reversed(range(16))]
ITERS = 10
T = 128
NB = M // T
TILES = [(i, j) for i in range(NB) for j in range(i + 1, NB)] + [(i, i) for i in range(0, NB, 2)]
HALF = len(TILES) // 2
ROWS = HALF * T
HEAD = 8
BLOCK_SIZE = 32
BLOCKS = 8
STRIP = ROWS // BLOCK_SIZE
SLAB = STRIP + HEAD
SPLIT = 512
GROUP = 16
MEM = ("zo", "zi", "core")
PLANE = ("y", "x")
BLOCK = ("zi", "y", "x")


def above_mask():
    return lax.broadcasted_iota(jnp.int32, (T, T), 0) < lax.broadcasted_iota(jnp.int32, (T, T), 1)


def eye_mask():
    return lax.broadcasted_iota(jnp.int32, (T, T), 0) == lax.broadcasted_iota(jnp.int32, (T, T), 1)


def split_kernel(ensemble_ref, out_ref):
    count, _, cells = out_ref.shape
    for d in range(count):
        out_ref[d] = ensemble_ref[:, d * cells:(d + 1) * cells]


def join_kernel(blocks_ref, out_ref, sems):
    count, _, cells = blocks_ref.shape
    copies = [
        pltpu.make_async_copy(blocks_ref.at[d], out_ref.at[:, d * cells:(d + 1) * cells], sems.at[d])
        for d in range(count)
    ]
    for copy in copies:
        copy.start()
    for copy in copies:
        copy.wait()


def split_cells(ensemble, shape):
    return pl.pallas_call(
        split_kernel,
        out_shape=jax.ShapeDtypeStruct(shape, ensemble.dtype),
        in_specs=[pl.BlockSpec(memory_space=pltpu.VMEM)],
        out_specs=pl.BlockSpec(memory_space=pltpu.VMEM),
        compiler_params=pltpu.CompilerParams(vmem_limit_bytes=8 << 20),
        name="split",
    )(ensemble)


def join_cells(blocks, shape):
    return pl.pallas_call(
        join_kernel,
        out_shape=jax.ShapeDtypeStruct(shape, blocks.dtype),
        in_specs=[pl.BlockSpec(memory_space=pltpu.VMEM)],
        out_specs=pl.BlockSpec(memory_space=pltpu.HBM),
        scratch_shapes=[pltpu.SemaphoreType.DMA((blocks.shape[0],))],
        compiler_params=pltpu.CompilerParams(vmem_limit_bytes=8 << 20),
        name="join",
    )(blocks)


def distance_kernel(relaid_ref, keep_ref, send_ref, packed):
    core = lax.axis_index("core")
    eye = eye_mask()
    norm_row = {}
    sums = jnp.zeros((8, T), jnp.float32)
    largest = jnp.zeros((8, T), jnp.float32)
    for start in reversed(range(0, NB, 2)):
        strip = lax.dot_general(
            relaid_ref[start * T:(start + 2) * T, :], relaid_ref[start * T:, :],
            (((1,), (1,)), ((), ())), preferred_element_type=jnp.float32,
        )
        values = {}
        for i in (start + 1, start):
            rows = slice((i - start) * T, (i - start + 1) * T)
            own = jnp.where(eye, strip[rows, rows], 0.0)
            norm_row[i] = jnp.sum(own, axis=0, keepdims=True)
            norm_col = jnp.sum(own, axis=1, keepdims=True)
            for j in range(i, NB):
                gram = strip[rows, (j - start) * T:(j - start + 1) * T]
                values[i, j] = norm_col + norm_row[j] - 2.0 * gram
        second = values.pop((start + 1, start + 1))
        values[start, start] = jnp.where(above_mask(), values[start, start], second)
        for tile, value in values.items():
            half, slot = divmod(TILES.index(tile), HALF)
            packed[half, slot * T:(slot + 1) * T, :] = value
            folded = value.reshape(T // 8, 8, T)
            largest = jnp.maximum(largest, jnp.max(folded, axis=0))
            sums += jnp.sum(folded, axis=0)
    total = jnp.broadcast_to(2.0 * jnp.sum(sums, keepdims=True), (1, T))
    bound = jnp.broadcast_to(jnp.max(largest, keepdims=True), (1, T))
    power, scale = scaling(bound)
    row = lax.broadcasted_iota(jnp.int32, (HEAD, T), 0)
    keep_ref[:ROWS, :] = packed[core]
    keep_ref[ROWS:, :] = jnp.where(row == 0, total, jnp.where(row == 1, bound, 0.0))
    send_ref[:ROWS, :] = packed[1 - core] * scale
    send_ref[ROWS:, :] = tail_rows(power, scale, total)


def partial_distances(relaid):
    shape = jax.ShapeDtypeStruct((ROWS + HEAD, T), jnp.float32)
    vmem = pl.BlockSpec(memory_space=pltpu.VMEM)
    return pl.pallas_call(
        distance_kernel,
        out_shape=(shape, shape),
        in_specs=[vmem],
        out_specs=(vmem, vmem),
        scratch_shapes=[pltpu.VMEM((2, ROWS, T), jnp.float32)],
        compiler_params=pltpu.CompilerParams(vmem_limit_bytes=32 << 20),
        name="distances",
    )(relaid)


def scaling(bound):
    power = jnp.floor(15.0 - jnp.log2(jnp.maximum(bound, 1e-30)))
    return power, jnp.exp2(power)


def tail_rows(power, scale, total):
    share = total * scale * 2.0**-20
    high = share.astype(jnp.bfloat16).astype(jnp.float32)
    middle = (share - high).astype(jnp.bfloat16).astype(jnp.float32)
    low = share - high - middle
    row = lax.broadcasted_iota(jnp.int32, (HEAD, T), 0)
    tail = jnp.zeros((HEAD, T), jnp.float32)
    for index, value in enumerate((power, high, middle, low)):
        tail = jnp.where(row == index, value, tail)
    return tail


def tail_total(tail, inverse):
    return (tail[1:2, :] + tail[2:3, :] + tail[3:4, :]) * inverse * 2.0**20


def summed(parts_ref):
    acc = jnp.zeros((STRIP, T), jnp.float32)
    total = jnp.zeros((1, T), jnp.float32)
    for p in range(parts_ref.shape[0]):
        tail = parts_ref[p, STRIP:, :]
        inverse = jnp.exp2(-tail[0:1, :])
        acc += parts_ref[p, :STRIP, :] * inverse
        total += tail_total(tail, inverse)
    return acc, total


def pack_kernel(keep_ref, recv_ref, out_ref):
    other = recv_ref[ROWS:, :]
    inverse = jnp.exp2(-other[0:1, :])
    total = keep_ref[ROWS:ROWS + 1, :] + tail_total(other, inverse)
    power, scale = scaling(keep_ref[ROWS + 1:ROWS + 2, :] + jnp.exp2(15.0 - other[0:1, :]))
    tail = tail_rows(power, scale, total)
    for p in range(BLOCK_SIZE):
        rows = slice(p * STRIP, (p + 1) * STRIP)
        out_ref[p, :STRIP, :] = (keep_ref[rows, :] + recv_ref[rows, :] * inverse) * scale
        out_ref[p, STRIP:, :] = tail


def strip_kernel(parts_ref, out_ref):
    acc, total = summed(parts_ref)
    power, scale = scaling(jnp.maximum(jnp.max(acc, keepdims=True), total * 2.0**-20))
    tail = tail_rows(power, scale, total)
    acc = acc * scale
    for g in range(BLOCKS):
        out_ref[g, :STRIP, :] = acc
        out_ref[g, STRIP:, :] = tail


def entries_kernel(parts_ref, out_ref):
    acc, total = summed(parts_ref)
    mean = total / (M * (M - 1))
    entries = jnp.exp(acc * (-1.0 / (0.08 * mean))).astype(jnp.bfloat16)
    for p in range(BLOCK_SIZE):
        out_ref[p, :, :] = entries


def small_call(body, shape, dtype, name):
    return pl.pallas_call(
        body,
        out_shape=jax.ShapeDtypeStruct(shape, dtype),
        compiler_params=pltpu.CompilerParams(vmem_limit_bytes=16 << 20),
        name=name,
    )


def analysis_kernel(own_ref, other_ref, logw_ref, relaid_ref, out_ref,
                    packed, kern_a, kern_at, kern_b, weight, scale, coup):
    core = lax.axis_index("core")
    for p in range(BLOCK_SIZE):
        rows = slice(p * STRIP, (p + 1) * STRIP)
        packed[core, rows, :] = own_ref[p].astype(jnp.float32)
        packed[1 - core, rows, :] = other_ref[p].astype(jnp.float32)

    def place(i, j, value):
        cols = slice(j * T, (j + 1) * T)
        if i * T < SPLIT:
            kern_a[i * T:(i + 1) * T, cols] = value.astype(jnp.bfloat16)
        else:
            kern_b[i * T - SPLIT:(i + 1) * T - SPLIT, cols] = value
        if j * T < SPLIT:
            kern_at[i * T:(i + 1) * T, cols] = value.astype(jnp.bfloat16)

    for tile, (i, j) in enumerate(TILES):
        half, slot = divmod(tile, HALF)
        value = packed[half, slot * T:(slot + 1) * T, :]
        if i == j:
            above = above_mask()
            place(i, i, jnp.where(above, value, value.T))
            place(i + 1, i + 1, jnp.where(above, value.T, value))
        else:
            place(i, j, value)
            place(j, i, value.T)

    eye = eye_mask()

    def to_column(row):
        return jnp.broadcast_to(jnp.sum(jnp.where(eye, row, 0.0), axis=1, keepdims=True), (T, T))

    logw = logw_ref[...]
    expw = jnp.exp(logw - jnp.max(logw, axis=1, keepdims=True))
    weights = expw / jnp.sum(expw, axis=1, keepdims=True)
    weights = jnp.concatenate([weights[:, k * OWN:(k + 1) * OWN] for k in ORDER], axis=1)
    for i in range(SPLIT // T, NB):
        weight[i * T - SPLIT:(i + 1) * T - SPLIT, :] = to_column(weights[:, i * T:(i + 1) * T])

    def product(vector, matrix):
        first = vector.astype(jnp.bfloat16).astype(jnp.float32)
        second = (vector - first).astype(jnp.bfloat16).astype(jnp.float32)
        third = vector - first - second
        row = lax.broadcasted_iota(jnp.int32, (16, vector.shape[1]), 0)
        parts = jnp.where(row == 0, first, jnp.where(row == 1, second, jnp.where(row == 2, third, 0.0)))
        sums = jnp.dot(parts.astype(jnp.bfloat16), matrix, preferred_element_type=jnp.float32)
        return sums[0:1, :] + sums[1:2, :] + sums[2:3, :]

    def sweep(step, scales):
        scale_col = scales[1]
        scale_a = weights[:, :SPLIT] / product(scale_col, kern_at[...])
        from_a = product(scale_a, kern_a[...])
        wide = [jnp.broadcast_to(scale_col[:, l * T:(l + 1) * T], (8, T)) for l in range(NB)]
        sums = [jnp.zeros((8, T), jnp.float32) for _ in range(NB)]
        for base in range(0, M - SPLIT, 8 * GROUP):
            row_scale = []
            for g in range(GROUP):
                rows = slice(base + 8 * g, base + 8 * g + 8)
                acc = kern_b[rows, 0:T] * wide[0]
                for l in range(1, NB):
                    acc += kern_b[rows, l * T:(l + 1) * T] * wide[l]
                r = weight[rows, :] / jnp.sum(acc, axis=1, keepdims=True)
                scale[rows, :] = r
                row_scale.append(r)
            for g in range(GROUP):
                rows = slice(base + 8 * g, base + 8 * g + 8)
                for l in range(NB):
                    sums[l] += kern_b[rows, l * T:(l + 1) * T] * row_scale[g]
        from_b = jnp.concatenate([jnp.sum(s, axis=0, keepdims=True) for s in sums], axis=1)
        return scale_a, (1.0 / M) / (from_a + from_b)

    start = (weights[:, :SPLIT], jnp.ones((1, M), jnp.float32))
    scale_a, scale_col = lax.fori_loop(0, ITERS, sweep, start)

    scale_row = [M * scale_a[:, i * T:(i + 1) * T] for i in range(SPLIT // T)]
    for i in range(SPLIT // T, NB):
        block = scale[i * T - SPLIT:(i + 1) * T - SPLIT, :]
        scale_row.append(M * jnp.sum(jnp.where(eye, block, 0.0), axis=0, keepdims=True))
    for j in range(NB):
        rows = slice(j * T, (j + 1) * T)
        column = to_column(scale_col[:, rows])
        for i in range(NB):
            cols = slice(i * T, (i + 1) * T)
            if j * T < SPLIT:
                value = kern_a[rows, cols].astype(jnp.float32)
            else:
                value = kern_b[j * T - SPLIT:(j + 1) * T - SPLIT, cols]
            coup[rows, cols] = (scale_row[i] * value * column).astype(jnp.bfloat16)
    for j in range(0, NB, 2):
        mixed = jnp.dot(
            coup[j * T:(j + 2) * T, :], relaid_ref[...], preferred_element_type=jnp.float32
        )
        out_ref[j * T:(j + 2) * T, :] = mixed.astype(jnp.bfloat16)


def analysis_members(own, other, log_weights, relaid):
    vmem = pl.BlockSpec(memory_space=pltpu.VMEM)
    return pl.pallas_call(
        analysis_kernel,
        out_shape=jax.ShapeDtypeStruct(relaid.shape, jnp.bfloat16),
        in_specs=[vmem, vmem, vmem, vmem],
        out_specs=vmem,
        scratch_shapes=[
            pltpu.VMEM((2, ROWS, T), jnp.float32),
            pltpu.VMEM((SPLIT, M), jnp.bfloat16),
            pltpu.VMEM((M, SPLIT), jnp.bfloat16),
            pltpu.VMEM((M - SPLIT, M), jnp.float32),
            pltpu.VMEM((M - SPLIT, T), jnp.float32),
            pltpu.VMEM((M - SPLIT, T), jnp.float32),
            pltpu.VMEM((M, M), jnp.bfloat16),
        ],
        compiler_params=pltpu.CompilerParams(vmem_limit_bytes=40 << 20),
        name="analysis",
    )(own, other, log_weights, relaid)


def exchange(values, axes):
    return lax.all_to_all(values, axes, 0, 0, tiled=True)


def ordered_exchange(values, axes, order):
    return lax.all_to_all(values, axes, 0, 0, tiled=True, axis_index_groups=[order])


def per_device(ensemble, log_weights):
    swap = [(0, 1), (1, 0)]
    rows, cells = ensemble.shape
    count = M // rows
    shape = (count, rows, cells // count)
    blocks = split_cells(ensemble, shape)
    relaid = ordered_exchange(blocks, MEM, ORDER).reshape(M, cells // count)
    keep, send = partial_distances(relaid)
    recv = lax.ppermute(send.astype(jnp.float16), "core", swap).astype(jnp.float32)
    slabs = small_call(pack_kernel, (BLOCK_SIZE, SLAB, T), jnp.float32, "pack")(keep, recv)
    parts = exchange(slabs.astype(jnp.float16), BLOCK).astype(jnp.float32)
    strips = small_call(strip_kernel, (BLOCKS, SLAB, T), jnp.float32, "strip")(parts)
    parts = ordered_exchange(strips.astype(jnp.float16), "zo", list(range(BLOCKS))[::-1]).astype(jnp.float32)
    entries = small_call(entries_kernel, (BLOCK_SIZE, STRIP, T), jnp.bfloat16, "entries")(parts)
    own = exchange(entries, BLOCK)
    other = lax.ppermute(own, "core", swap)
    mixed = analysis_members(own, other, log_weights.reshape(1, M), relaid)
    blocks = ordered_exchange(mixed.reshape(shape), MEM, ORDER)
    return join_cells(blocks, ensemble.shape)


def solution(mesh):
    fine = Mesh(mesh.devices.reshape(8, 2, 2, 4, 4), ("zo", "zi", "core", "y", "x"))
    return jax.shard_map(
        per_device,
        mesh=fine,
        in_specs=(P(MEM, PLANE), P()),
        out_specs=P(MEM, PLANE),
        check_vma=False,
    )
```

```python
import jax
import jax.numpy as jnp
from jax import lax
from jax.experimental import pallas as pl
from jax.experimental.pallas import tpu as pltpu
from jax.sharding import Mesh
from jax.sharding import PartitionSpec as P

M = 1024
OWN = 32
ORDER = [2 * z + core for core in (1, 0) for z in reversed(range(16))]
ITERS = 10
T = 128
NB = M // T
TILES = [(i, j) for i in range(NB) for j in range(i + 1, NB)] + [(i, i) for i in range(0, NB, 2)]
HALF = len(TILES) // 2
ROWS = HALF * T
HEAD = 8
BLOCK_SIZE = 32
BLOCKS = 8
STRIP = ROWS // BLOCK_SIZE
SLAB = STRIP + HEAD
SPLIT = 512
GROUP = 16
MEM = ("zo", "zi", "core")
PLANE = ("y", "x")
BLOCK = ("zi", "y", "x")


def above_mask():
    return lax.broadcasted_iota(jnp.int32, (T, T), 0) < lax.broadcasted_iota(jnp.int32, (T, T), 1)


def eye_mask():
    return lax.broadcasted_iota(jnp.int32, (T, T), 0) == lax.broadcasted_iota(jnp.int32, (T, T), 1)


def split_kernel(ensemble_ref, out_ref, sems):
    count, _, cells = out_ref.shape
    copies = [
        pltpu.make_async_copy(ensemble_ref.at[:, d * cells:(d + 1) * cells], out_ref.at[d], sems.at[d])
        for d in range(count)
    ]
    for copy in copies:
        copy.start()
    for copy in copies:
        copy.wait()


def join_kernel(blocks_ref, out_ref, sems):
    count, _, cells = blocks_ref.shape
    copies = [
        pltpu.make_async_copy(blocks_ref.at[d], out_ref.at[:, d * cells:(d + 1) * cells], sems.at[d])
        for d in range(count)
    ]
    for copy in copies:
        copy.start()
    for copy in copies:
        copy.wait()


def split_cells(ensemble, shape):
    return pl.pallas_call(
        split_kernel,
        out_shape=jax.ShapeDtypeStruct(shape, ensemble.dtype),
        in_specs=[pl.BlockSpec(memory_space=pltpu.HBM)],
        out_specs=pl.BlockSpec(memory_space=pltpu.VMEM),
        scratch_shapes=[pltpu.SemaphoreType.DMA((shape[0],))],
        compiler_params=pltpu.CompilerParams(vmem_limit_bytes=52 << 20),
        name="split",
    )(ensemble)


def join_cells(blocks, shape):
    return pl.pallas_call(
        join_kernel,
        out_shape=jax.ShapeDtypeStruct(shape, blocks.dtype),
        in_specs=[pl.BlockSpec(memory_space=pltpu.VMEM)],
        out_specs=pl.BlockSpec(memory_space=pltpu.HBM),
        scratch_shapes=[pltpu.SemaphoreType.DMA((blocks.shape[0],))],
        compiler_params=pltpu.CompilerParams(vmem_limit_bytes=8 << 20),
        name="join",
    )(blocks)


def distance_kernel(relaid_ref, keep_ref, send_ref, packed):
    core = lax.axis_index("core")
    eye = eye_mask()
    norm_row = {}
    sums = jnp.zeros((8, T), jnp.float32)
    largest = jnp.zeros((8, T), jnp.float32)
    for start in reversed(range(0, NB, 2)):
        strip = lax.dot_general(
            relaid_ref[start * T:(start + 2) * T, :], relaid_ref[start * T:, :],
            (((1,), (1,)), ((), ())), preferred_element_type=jnp.float32,
        )
        values = {}
        for i in (start + 1, start):
            rows = slice((i - start) * T, (i - start + 1) * T)
            own = jnp.where(eye, strip[rows, rows], 0.0)
            norm_row[i] = jnp.sum(own, axis=0, keepdims=True)
            norm_col = jnp.sum(own, axis=1, keepdims=True)
            for j in range(i, NB):
                gram = strip[rows, (j - start) * T:(j - start + 1) * T]
                values[i, j] = norm_col + norm_row[j] - 2.0 * gram
        second = values.pop((start + 1, start + 1))
        values[start, start] = jnp.where(above_mask(), values[start, start], second)
        for tile, value in values.items():
            half, slot = divmod(TILES.index(tile), HALF)
            packed[half, slot * T:(slot + 1) * T, :] = value
            folded = value.reshape(T // 8, 8, T)
            largest = jnp.maximum(largest, jnp.max(folded, axis=0))
            sums += jnp.sum(folded, axis=0)
    total = jnp.broadcast_to(2.0 * jnp.sum(sums, keepdims=True), (1, T))
    bound = jnp.broadcast_to(jnp.max(largest, keepdims=True), (1, T))
    power, scale = scaling(bound)
    row = lax.broadcasted_iota(jnp.int32, (HEAD, T), 0)
    keep_ref[:ROWS, :] = packed[core]
    keep_ref[ROWS:, :] = jnp.where(row == 0, total, jnp.where(row == 1, bound, 0.0))
    send_ref[:ROWS, :] = packed[1 - core] * scale
    send_ref[ROWS:, :] = tail_rows(power, scale, total)


def partial_distances(relaid):
    shape = jax.ShapeDtypeStruct((ROWS + HEAD, T), jnp.float32)
    vmem = pl.BlockSpec(memory_space=pltpu.VMEM)
    return pl.pallas_call(
        distance_kernel,
        out_shape=(shape, shape),
        in_specs=[vmem],
        out_specs=(vmem, vmem),
        scratch_shapes=[pltpu.VMEM((2, ROWS, T), jnp.float32)],
        compiler_params=pltpu.CompilerParams(vmem_limit_bytes=32 << 20),
        name="distances",
    )(relaid)


def scaling(bound):
    power = jnp.floor(15.0 - jnp.log2(jnp.maximum(bound, 1e-30)))
    return power, jnp.exp2(power)


def tail_rows(power, scale, total):
    share = total * scale * 2.0**-20
    high = share.astype(jnp.bfloat16).astype(jnp.float32)
    middle = (share - high).astype(jnp.bfloat16).astype(jnp.float32)
    low = share - high - middle
    row = lax.broadcasted_iota(jnp.int32, (HEAD, T), 0)
    tail = jnp.zeros((HEAD, T), jnp.float32)
    for index, value in enumerate((power, high, middle, low)):
        tail = jnp.where(row == index, value, tail)
    return tail


def tail_total(tail, inverse):
    return (tail[1:2, :] + tail[2:3, :] + tail[3:4, :]) * inverse * 2.0**20


def summed(parts_ref):
    acc = jnp.zeros((STRIP, T), jnp.float32)
    total = jnp.zeros((1, T), jnp.float32)
    for p in range(parts_ref.shape[0]):
        tail = parts_ref[p, STRIP:, :]
        inverse = jnp.exp2(-tail[0:1, :])
        acc += parts_ref[p, :STRIP, :] * inverse
        total += tail_total(tail, inverse)
    return acc, total


def pack_kernel(keep_ref, recv_ref, out_ref):
    other = recv_ref[ROWS:, :]
    inverse = jnp.exp2(-other[0:1, :])
    total = keep_ref[ROWS:ROWS + 1, :] + tail_total(other, inverse)
    power, scale = scaling(keep_ref[ROWS + 1:ROWS + 2, :] + jnp.exp2(15.0 - other[0:1, :]))
    tail = tail_rows(power, scale, total)
    for p in range(BLOCK_SIZE):
        rows = slice(p * STRIP, (p + 1) * STRIP)
        out_ref[p, :STRIP, :] = (keep_ref[rows, :] + recv_ref[rows, :] * inverse) * scale
        out_ref[p, STRIP:, :] = tail


def strip_kernel(parts_ref, out_ref):
    acc, total = summed(parts_ref)
    power, scale = scaling(jnp.maximum(jnp.max(acc, keepdims=True), total * 2.0**-20))
    tail = tail_rows(power, scale, total)
    acc = acc * scale
    for g in range(BLOCKS):
        out_ref[g, :STRIP, :] = acc
        out_ref[g, STRIP:, :] = tail


def entries_kernel(parts_ref, out_ref):
    acc, total = summed(parts_ref)
    mean = total / (M * (M - 1))
    entries = jnp.exp(acc * (-1.0 / (0.08 * mean))).astype(jnp.bfloat16)
    for p in range(BLOCK_SIZE):
        out_ref[p, :, :] = entries


def small_call(body, shape, dtype, name):
    return pl.pallas_call(
        body,
        out_shape=jax.ShapeDtypeStruct(shape, dtype),
        compiler_params=pltpu.CompilerParams(vmem_limit_bytes=16 << 20),
        name=name,
    )


def analysis_kernel(own_ref, other_ref, logw_ref, relaid_ref, out_ref,
                    packed, kern_a, kern_at, kern_b, weight, scale, coup):
    core = lax.axis_index("core")
    for p in range(BLOCK_SIZE):
        rows = slice(p * STRIP, (p + 1) * STRIP)
        packed[core, rows, :] = own_ref[p].astype(jnp.float32)
        packed[1 - core, rows, :] = other_ref[p].astype(jnp.float32)

    def place(i, j, value):
        cols = slice(j * T, (j + 1) * T)
        if i * T < SPLIT:
            kern_a[i * T:(i + 1) * T, cols] = value.astype(jnp.bfloat16)
        else:
            kern_b[i * T - SPLIT:(i + 1) * T - SPLIT, cols] = value
        if j * T < SPLIT:
            kern_at[i * T:(i + 1) * T, cols] = value.astype(jnp.bfloat16)

    for tile, (i, j) in enumerate(TILES):
        half, slot = divmod(tile, HALF)
        value = packed[half, slot * T:(slot + 1) * T, :]
        if i == j:
            above = above_mask()
            place(i, i, jnp.where(above, value, value.T))
            place(i + 1, i + 1, jnp.where(above, value.T, value))
        else:
            place(i, j, value)
            place(j, i, value.T)

    eye = eye_mask()

    def to_column(row):
        return jnp.broadcast_to(jnp.sum(jnp.where(eye, row, 0.0), axis=1, keepdims=True), (T, T))

    logw = logw_ref[...]
    expw = jnp.exp(logw - jnp.max(logw, axis=1, keepdims=True))
    weights = expw / jnp.sum(expw, axis=1, keepdims=True)
    weights = jnp.concatenate([weights[:, k * OWN:(k + 1) * OWN] for k in ORDER], axis=1)
    for i in range(SPLIT // T, NB):
        weight[i * T - SPLIT:(i + 1) * T - SPLIT, :] = to_column(weights[:, i * T:(i + 1) * T])

    def product(vector, matrix):
        first = vector.astype(jnp.bfloat16).astype(jnp.float32)
        second = (vector - first).astype(jnp.bfloat16).astype(jnp.float32)
        third = vector - first - second
        row = lax.broadcasted_iota(jnp.int32, (16, vector.shape[1]), 0)
        parts = jnp.where(row == 0, first, jnp.where(row == 1, second, jnp.where(row == 2, third, 0.0)))
        sums = jnp.dot(parts.astype(jnp.bfloat16), matrix, preferred_element_type=jnp.float32)
        return sums[0:1, :] + sums[1:2, :] + sums[2:3, :]

    def sweep(step, scales):
        scale_col = scales[1]
        scale_a = weights[:, :SPLIT] / product(scale_col, kern_at[...])
        from_a = product(scale_a, kern_a[...])
        wide = [jnp.broadcast_to(scale_col[:, l * T:(l + 1) * T], (8, T)) for l in range(NB)]
        sums = [jnp.zeros((8, T), jnp.float32) for _ in range(NB)]
        for base in range(0, M - SPLIT, 8 * GROUP):
            row_scale = []
            for g in range(GROUP):
                rows = slice(base + 8 * g, base + 8 * g + 8)
                acc = kern_b[rows, 0:T] * wide[0]
                for l in range(1, NB):
                    acc += kern_b[rows, l * T:(l + 1) * T] * wide[l]
                r = weight[rows, :] / jnp.sum(acc, axis=1, keepdims=True)
                scale[rows, :] = r
                row_scale.append(r)
            for g in range(GROUP):
                rows = slice(base + 8 * g, base + 8 * g + 8)
                for l in range(NB):
                    sums[l] += kern_b[rows, l * T:(l + 1) * T] * row_scale[g]
        from_b = jnp.concatenate([jnp.sum(s, axis=0, keepdims=True) for s in sums], axis=1)
        return scale_a, (1.0 / M) / (from_a + from_b)

    start = (weights[:, :SPLIT], jnp.ones((1, M), jnp.float32))
    scale_a, scale_col = lax.fori_loop(0, ITERS, sweep, start)

    scale_row = [M * scale_a[:, i * T:(i + 1) * T] for i in range(SPLIT // T)]
    for i in range(SPLIT // T, NB):
        block = scale[i * T - SPLIT:(i + 1) * T - SPLIT, :]
        scale_row.append(M * jnp.sum(jnp.where(eye, block, 0.0), axis=0, keepdims=True))
    for j in range(NB):
        rows = slice(j * T, (j + 1) * T)
        column = to_column(scale_col[:, rows])
        for i in range(NB):
            cols = slice(i * T, (i + 1) * T)
            if j * T < SPLIT:
                value = kern_a[rows, cols].astype(jnp.float32)
            else:
                value = kern_b[j * T - SPLIT:(j + 1) * T - SPLIT, cols]
            coup[rows, cols] = (scale_row[i] * value * column).astype(jnp.bfloat16)
    for j in range(0, NB, 2):
        mixed = jnp.dot(
            coup[j * T:(j + 2) * T, :], relaid_ref[...], preferred_element_type=jnp.float32
        )
        out_ref[j * T:(j + 2) * T, :] = mixed.astype(jnp.bfloat16)


def analysis_members(own, other, log_weights, relaid):
    vmem = pl.BlockSpec(memory_space=pltpu.VMEM)
    return pl.pallas_call(
        analysis_kernel,
        out_shape=jax.ShapeDtypeStruct(relaid.shape, jnp.bfloat16),
        in_specs=[vmem, vmem, vmem, vmem],
        out_specs=vmem,
        scratch_shapes=[
            pltpu.VMEM((2, ROWS, T), jnp.float32),
            pltpu.VMEM((SPLIT, M), jnp.bfloat16),
            pltpu.VMEM((M, SPLIT), jnp.bfloat16),
            pltpu.VMEM((M - SPLIT, M), jnp.float32),
            pltpu.VMEM((M - SPLIT, T), jnp.float32),
            pltpu.VMEM((M - SPLIT, T), jnp.float32),
            pltpu.VMEM((M, M), jnp.bfloat16),
        ],
        compiler_params=pltpu.CompilerParams(vmem_limit_bytes=40 << 20),
        name="analysis",
    )(own, other, log_weights, relaid)


def exchange(values, axes):
    return lax.all_to_all(values, axes, 0, 0, tiled=True)


def ordered_exchange(values, axes, order):
    return lax.all_to_all(values, axes, 0, 0, tiled=True, axis_index_groups=[order])


def per_device(ensemble, log_weights):
    swap = [(0, 1), (1, 0)]
    rows, cells = ensemble.shape
    count = M // rows
    shape = (count, rows, cells // count)
    blocks = split_cells(ensemble, shape)
    relaid = ordered_exchange(blocks, MEM, ORDER).reshape(M, cells // count)
    keep, send = partial_distances(relaid)
    recv = lax.ppermute(send.astype(jnp.float16), "core", swap).astype(jnp.float32)
    slabs = small_call(pack_kernel, (BLOCK_SIZE, SLAB, T), jnp.float32, "pack")(keep, recv)
    parts = exchange(slabs.astype(jnp.float16), BLOCK).astype(jnp.float32)
    strips = small_call(strip_kernel, (BLOCKS, SLAB, T), jnp.float32, "strip")(parts)
    parts = ordered_exchange(strips.astype(jnp.float16), "zo", list(range(BLOCKS))[::-1]).astype(jnp.float32)
    entries = small_call(entries_kernel, (BLOCK_SIZE, STRIP, T), jnp.bfloat16, "entries")(parts)
    own = exchange(entries, BLOCK)
    other = lax.ppermute(own, "core", swap)
    mixed = analysis_members(own, other, log_weights.reshape(1, M), relaid)
    blocks = ordered_exchange(mixed.reshape(shape), MEM, ORDER)
    return join_cells(blocks, ensemble.shape)


def solution(mesh):
    fine = Mesh(mesh.devices.reshape(8, 2, 2, 4, 4), ("zo", "zi", "core", "y", "x"))
    return jax.shard_map(
        per_device,
        mesh=fine,
        in_specs=(P(MEM, PLANE), P()),
        out_specs=P(MEM, PLANE),
        check_vma=False,
    )
```

```python
import jax
import jax.numpy as jnp
from jax import lax
from jax.experimental import pallas as pl
from jax.experimental.pallas import tpu as pltpu
from jax.sharding import Mesh
from jax.sharding import PartitionSpec as P

M = 1024
OWN = 32
ORDER = [2 * z + core for core in (1, 0) for z in reversed(range(16))]
ITERS = 10
T = 128
NB = M // T
TILES = [(i, j) for i in range(NB) for j in range(i + 1, NB)] + [(i, i) for i in range(0, NB, 2)]
HALF = len(TILES) // 2
ROWS = HALF * T
HEAD = 8
BLOCK_SIZE = 32
BLOCKS = 8
STRIP = ROWS // BLOCK_SIZE
SLAB = STRIP + HEAD
SPLIT = 512
GROUP = 16
MEM = ("zo", "zi", "core")
PLANE = ("y", "x")
BLOCK = ("zi", "y", "x")


def above_mask():
    return lax.broadcasted_iota(jnp.int32, (T, T), 0) < lax.broadcasted_iota(jnp.int32, (T, T), 1)


def eye_mask():
    return lax.broadcasted_iota(jnp.int32, (T, T), 0) == lax.broadcasted_iota(jnp.int32, (T, T), 1)


def split_kernel(ensemble_ref, out_ref):
    count, _, cells = out_ref.shape
    for d in range(count):
        out_ref[d] = ensemble_ref[:, d * cells:(d + 1) * cells]


def split_cells(ensemble, shape):
    return pl.pallas_call(
        split_kernel,
        out_shape=jax.ShapeDtypeStruct(shape, ensemble.dtype),
        in_specs=[pl.BlockSpec(memory_space=pltpu.VMEM)],
        out_specs=pl.BlockSpec(memory_space=pltpu.VMEM),
        compiler_params=pltpu.CompilerParams(vmem_limit_bytes=8 << 20),
        name="split",
    )(ensemble)


def distance_kernel(relaid_ref, keep_ref, send_ref, packed):
    core = lax.axis_index("core")
    eye = eye_mask()
    norm_row = {}
    sums = jnp.zeros((8, T), jnp.float32)
    largest = jnp.zeros((8, T), jnp.float32)
    for start in reversed(range(0, NB, 2)):
        strip = lax.dot_general(
            relaid_ref[start * T:(start + 2) * T, :], relaid_ref[start * T:, :],
            (((1,), (1,)), ((), ())), preferred_element_type=jnp.float32,
        )
        values = {}
        for i in (start + 1, start):
            rows = slice((i - start) * T, (i - start + 1) * T)
            own = jnp.where(eye, strip[rows, rows], 0.0)
            norm_row[i] = jnp.sum(own, axis=0, keepdims=True)
            norm_col = jnp.sum(own, axis=1, keepdims=True)
            for j in range(i, NB):
                gram = strip[rows, (j - start) * T:(j - start + 1) * T]
                values[i, j] = norm_col + norm_row[j] - 2.0 * gram
        second = values.pop((start + 1, start + 1))
        values[start, start] = jnp.where(above_mask(), values[start, start], second)
        for tile, value in values.items():
            half, slot = divmod(TILES.index(tile), HALF)
            packed[half, slot * T:(slot + 1) * T, :] = value
            folded = value.reshape(T // 8, 8, T)
            largest = jnp.maximum(largest, jnp.max(folded, axis=0))
            sums += jnp.sum(folded, axis=0)
    total = jnp.broadcast_to(2.0 * jnp.sum(sums, keepdims=True), (1, T))
    bound = jnp.broadcast_to(jnp.max(largest, keepdims=True), (1, T))
    power, scale = scaling(bound)
    row = lax.broadcasted_iota(jnp.int32, (HEAD, T), 0)
    keep_ref[:ROWS, :] = packed[core]
    keep_ref[ROWS:, :] = jnp.where(row == 0, total, jnp.where(row == 1, bound, 0.0))
    send_ref[:ROWS, :] = packed[1 - core] * scale
    send_ref[ROWS:, :] = tail_rows(power, scale, total)


def partial_distances(relaid):
    shape = jax.ShapeDtypeStruct((ROWS + HEAD, T), jnp.float32)
    vmem = pl.BlockSpec(memory_space=pltpu.VMEM)
    return pl.pallas_call(
        distance_kernel,
        out_shape=(shape, shape),
        in_specs=[vmem],
        out_specs=(vmem, vmem),
        scratch_shapes=[pltpu.VMEM((2, ROWS, T), jnp.float32)],
        compiler_params=pltpu.CompilerParams(vmem_limit_bytes=32 << 20),
        name="distances",
    )(relaid)


def scaling(bound):
    power = jnp.floor(15.0 - jnp.log2(jnp.maximum(bound, 1e-30)))
    return power, jnp.exp2(power)


def tail_rows(power, scale, total):
    share = total * scale * 2.0**-20
    high = share.astype(jnp.bfloat16).astype(jnp.float32)
    middle = (share - high).astype(jnp.bfloat16).astype(jnp.float32)
    low = share - high - middle
    row = lax.broadcasted_iota(jnp.int32, (HEAD, T), 0)
    tail = jnp.zeros((HEAD, T), jnp.float32)
    for index, value in enumerate((power, high, middle, low)):
        tail = jnp.where(row == index, value, tail)
    return tail


def tail_total(tail, inverse):
    return (tail[1:2, :] + tail[2:3, :] + tail[3:4, :]) * inverse * 2.0**20


def summed(parts_ref):
    acc = jnp.zeros((STRIP, T), jnp.float32)
    total = jnp.zeros((1, T), jnp.float32)
    for p in range(parts_ref.shape[0]):
        tail = parts_ref[p, STRIP:, :]
        inverse = jnp.exp2(-tail[0:1, :])
        acc += parts_ref[p, :STRIP, :] * inverse
        total += tail_total(tail, inverse)
    return acc, total


def pack_kernel(keep_ref, recv_ref, out_ref):
    other = recv_ref[ROWS:, :]
    inverse = jnp.exp2(-other[0:1, :])
    total = keep_ref[ROWS:ROWS + 1, :] + tail_total(other, inverse)
    power, scale = scaling(keep_ref[ROWS + 1:ROWS + 2, :] + jnp.exp2(15.0 - other[0:1, :]))
    tail = tail_rows(power, scale, total)
    for p in range(BLOCK_SIZE):
        rows = slice(p * STRIP, (p + 1) * STRIP)
        out_ref[p, :STRIP, :] = (keep_ref[rows, :] + recv_ref[rows, :] * inverse) * scale
        out_ref[p, STRIP:, :] = tail


def strip_kernel(parts_ref, out_ref):
    acc, total = summed(parts_ref)
    power, scale = scaling(jnp.maximum(jnp.max(acc, keepdims=True), total * 2.0**-20))
    tail = tail_rows(power, scale, total)
    acc = acc * scale
    for g in range(BLOCKS):
        out_ref[g, :STRIP, :] = acc
        out_ref[g, STRIP:, :] = tail


def entries_kernel(parts_ref, out_ref):
    acc, total = summed(parts_ref)
    mean = total / (M * (M - 1))
    entries = jnp.exp(acc * (-1.0 / (0.08 * mean))).astype(jnp.bfloat16)
    for p in range(BLOCK_SIZE):
        out_ref[p, :, :] = entries


def small_call(body, shape, dtype, name):
    return pl.pallas_call(
        body,
        out_shape=jax.ShapeDtypeStruct(shape, dtype),
        compiler_params=pltpu.CompilerParams(vmem_limit_bytes=16 << 20),
        name=name,
    )


def analysis_kernel(own_ref, other_ref, logw_ref, relaid_ref, out_ref,
                    packed, kern_a, kern_at, kern_b, weight, scale, coup):
    core = lax.axis_index("core")
    for p in range(BLOCK_SIZE):
        rows = slice(p * STRIP, (p + 1) * STRIP)
        packed[core, rows, :] = own_ref[p].astype(jnp.float32)
        packed[1 - core, rows, :] = other_ref[p].astype(jnp.float32)

    def place(i, j, value):
        cols = slice(j * T, (j + 1) * T)
        if i * T < SPLIT:
            kern_a[i * T:(i + 1) * T, cols] = value.astype(jnp.bfloat16)
        else:
            kern_b[i * T - SPLIT:(i + 1) * T - SPLIT, cols] = value
        if j * T < SPLIT:
            kern_at[i * T:(i + 1) * T, cols] = value.astype(jnp.bfloat16)

    for tile, (i, j) in enumerate(TILES):
        half, slot = divmod(tile, HALF)
        value = packed[half, slot * T:(slot + 1) * T, :]
        if i == j:
            above = above_mask()
            place(i, i, jnp.where(above, value, value.T))
            place(i + 1, i + 1, jnp.where(above, value.T, value))
        else:
            place(i, j, value)
            place(j, i, value.T)

    eye = eye_mask()

    def to_column(row):
        return jnp.broadcast_to(jnp.sum(jnp.where(eye, row, 0.0), axis=1, keepdims=True), (T, T))

    logw = logw_ref[...]
    expw = jnp.exp(logw - jnp.max(logw, axis=1, keepdims=True))
    weights = expw / jnp.sum(expw, axis=1, keepdims=True)
    weights = jnp.concatenate([weights[:, k * OWN:(k + 1) * OWN] for k in ORDER], axis=1)
    for i in range(SPLIT // T, NB):
        weight[i * T - SPLIT:(i + 1) * T - SPLIT, :] = to_column(weights[:, i * T:(i + 1) * T])

    def product(vector, matrix):
        first = vector.astype(jnp.bfloat16).astype(jnp.float32)
        second = (vector - first).astype(jnp.bfloat16).astype(jnp.float32)
        third = vector - first - second
        row = lax.broadcasted_iota(jnp.int32, (16, vector.shape[1]), 0)
        parts = jnp.where(row == 0, first, jnp.where(row == 1, second, jnp.where(row == 2, third, 0.0)))
        sums = jnp.dot(parts.astype(jnp.bfloat16), matrix, preferred_element_type=jnp.float32)
        return sums[0:1, :] + sums[1:2, :] + sums[2:3, :]

    def sweep(step, scales):
        scale_col = scales[1]
        scale_a = weights[:, :SPLIT] / product(scale_col, kern_at[...])
        from_a = product(scale_a, kern_a[...])
        wide = [jnp.broadcast_to(scale_col[:, l * T:(l + 1) * T], (8, T)) for l in range(NB)]
        sums = [jnp.zeros((8, T), jnp.float32) for _ in range(NB)]
        for base in range(0, M - SPLIT, 8 * GROUP):
            row_scale = []
            for g in range(GROUP):
                rows = slice(base + 8 * g, base + 8 * g + 8)
                acc = kern_b[rows, 0:T] * wide[0]
                for l in range(1, NB):
                    acc += kern_b[rows, l * T:(l + 1) * T] * wide[l]
                r = weight[rows, :] / jnp.sum(acc, axis=1, keepdims=True)
                scale[rows, :] = r
                row_scale.append(r)
            for g in range(GROUP):
                rows = slice(base + 8 * g, base + 8 * g + 8)
                for l in range(NB):
                    sums[l] += kern_b[rows, l * T:(l + 1) * T] * row_scale[g]
        from_b = jnp.concatenate([jnp.sum(s, axis=0, keepdims=True) for s in sums], axis=1)
        return scale_a, (1.0 / M) / (from_a + from_b)

    start = (weights[:, :SPLIT], jnp.ones((1, M), jnp.float32))
    scale_a, scale_col = lax.fori_loop(0, ITERS, sweep, start)

    scale_row = [M * scale_a[:, i * T:(i + 1) * T] for i in range(SPLIT // T)]
    for i in range(SPLIT // T, NB):
        block = scale[i * T - SPLIT:(i + 1) * T - SPLIT, :]
        scale_row.append(M * jnp.sum(jnp.where(eye, block, 0.0), axis=0, keepdims=True))
    for j in range(NB):
        rows = slice(j * T, (j + 1) * T)
        column = to_column(scale_col[:, rows])
        for i in range(NB):
            cols = slice(i * T, (i + 1) * T)
            if j * T < SPLIT:
                value = kern_a[rows, cols].astype(jnp.float32)
            else:
                value = kern_b[j * T - SPLIT:(j + 1) * T - SPLIT, cols]
            coup[rows, cols] = (scale_row[i] * value * column).astype(jnp.bfloat16)
    for j in range(0, NB, 2):
        mixed = jnp.dot(
            coup[j * T:(j + 2) * T, :], relaid_ref[...], preferred_element_type=jnp.float32
        )
        out_ref[j * T:(j + 2) * T, :] = mixed.astype(jnp.bfloat16)


def analysis_members(own, other, log_weights, relaid):
    vmem = pl.BlockSpec(memory_space=pltpu.VMEM)
    return pl.pallas_call(
        analysis_kernel,
        out_shape=jax.ShapeDtypeStruct(relaid.shape, jnp.bfloat16),
        in_specs=[vmem, vmem, vmem, vmem],
        out_specs=vmem,
        scratch_shapes=[
            pltpu.VMEM((2, ROWS, T), jnp.float32),
            pltpu.VMEM((SPLIT, M), jnp.bfloat16),
            pltpu.VMEM((M, SPLIT), jnp.bfloat16),
            pltpu.VMEM((M - SPLIT, M), jnp.float32),
            pltpu.VMEM((M - SPLIT, T), jnp.float32),
            pltpu.VMEM((M - SPLIT, T), jnp.float32),
            pltpu.VMEM((M, M), jnp.bfloat16),
        ],
        compiler_params=pltpu.CompilerParams(vmem_limit_bytes=40 << 20),
        name="analysis",
    )(own, other, log_weights, relaid)


def exchange(values, axes):
    return lax.all_to_all(values, axes, 0, 0, tiled=True)


def ordered_exchange(values, axes, order):
    return lax.all_to_all(values, axes, 0, 0, tiled=True, axis_index_groups=[order])


def per_device(ensemble, log_weights):
    swap = [(0, 1), (1, 0)]
    rows, cells = ensemble.shape
    count = M // rows
    shape = (count, rows, cells // count)
    blocks = split_cells(ensemble, shape)
    relaid = ordered_exchange(blocks, MEM, ORDER).reshape(M, cells // count)
    keep, send = partial_distances(relaid)
    recv = lax.ppermute(send.astype(jnp.float16), "core", swap).astype(jnp.float32)
    slabs = small_call(pack_kernel, (BLOCK_SIZE, SLAB, T), jnp.float32, "pack")(keep, recv)
    parts = exchange(slabs.astype(jnp.float16), BLOCK).astype(jnp.float32)
    strips = small_call(strip_kernel, (BLOCKS, SLAB, T), jnp.float32, "strip")(parts)
    parts = ordered_exchange(strips.astype(jnp.float16), "zo", [7, 1, 2, 6, 5, 0, 3, 4]).astype(jnp.float32)
    entries = small_call(entries_kernel, (BLOCK_SIZE, STRIP, T), jnp.bfloat16, "entries")(parts)
    own = exchange(entries, BLOCK)
    other = lax.ppermute(own, "core", swap)
    mixed = analysis_members(own, other, log_weights.reshape(1, M), relaid)
    blocks = ordered_exchange(mixed.reshape(shape), MEM, ORDER)
    return blocks.transpose(1, 0, 2).reshape(ensemble.shape)


def solution(mesh):
    fine = Mesh(mesh.devices.reshape(8, 2, 2, 4, 4), ("zo", "zi", "core", "y", "x"))
    return jax.shard_map(
        per_device,
        mesh=fine,
        in_specs=(P(MEM, PLANE), P()),
        out_specs=P(MEM, PLANE),
        check_vma=False,
    )
```
